32 devices in a mesh: seq: 8 (over z, y), head: 4 (over x, core).
Axes of the slice: x: 2, y: 2, z: 4, core: 2. Of those that a mesh axis runs over, the one named last changes fastest.
Arguments:
- tokens: bfloat16 [16384, 1024], P('seq', 'head'), may hold values from -32 to 32
- buckets: int32 [128, 16], P('seq', 'head'), may hold values from 0 to 63, as said below
- w_shared: bfloat16 [1024, 1024], P(None, 'head'), may hold values from -3 to 3
- w_value: bfloat16 [1024, 1024], P(None, 'head'), may hold values from -0.1875 to 0.1875
- w_output: bfloat16 [1024, 1024], P(None, 'head'), may hold values from -0.1875 to 0.1875
Outputs:
- mixed_out: bfloat16 [16384, 1024], P('seq', 'head')
The draws below stay inside these ranges and needn't reach their ends.
Inputs may be any that keep to these rules, and one draw needn't show every extreme that they name: `buckets`: for each head, the ids 0 to 63 all occur. With the owner of a block in head h being its position in head h's ordering integer-divided by 16, exactly 16 blocks of each head fall to each owner, and over the 4 heads held by one device along `head` the 16 blocks held by one device along `seq` fall at most 8 to any one owner; 8 is reached in every draw.
All inputs are finite; a program needn't handle non-finite values.
Results may differ from the reference program's by a relative error of at most 0.012.
The reference program's roundings to bfloat16 on the way (of `shared`, `values`, `khat`, `weights` and `attention`) count: a program that leaves them out, or rounds other values in their place, can miss the bound.
Values may be sent and summed in bfloat16 or wider, within the bound.
A program may use at most 64 MiB of HBM per device.

```python
import jax
import jax.numpy as jnp
from jax import lax

D = 1024
H = 16
DH = 64
BLK = 128
HPD = 4
BLK_DEV = 16
TOTAL_BLOCKS = 128
TOKENS = 16384
NBUCK = 64
N_SEQ = 8
N_HEAD = 4


def draw_tokens(key, part):
    base = jnp.clip(jax.random.normal(jax.random.fold_in(key, 101), (TOKENS, D), jnp.float32), -6.0, 6.0)
    return base.astype(jnp.bfloat16)


def draw_w_shared(key, part):
    weight = jnp.clip(jax.random.normal(jax.random.fold_in(key, 201), (D, D), jnp.float32), -6.0, 6.0) * D ** (-0.5)
    weight = jnp.clip(weight, -3.0, 3.0)
    return weight.astype(jnp.bfloat16)


def draw_buckets(key, part):
    item_count = BLK_DEV * HPD
    span = max(item_count, N_SEQ)
    group_keys = jax.random.split(jax.random.fold_in(key, 11), N_HEAD)
    offsets = jax.vmap(lambda gkey: jax.random.permutation(gkey, span)[:item_count])(group_keys) % N_SEQ
    offsets = offsets.reshape(H, BLK_DEV).astype(jnp.int32)
    source = jnp.arange(N_SEQ, dtype=jnp.int32)
    owner_index = (source[None, :, None] + offsets[:, None, :]) % N_SEQ
    senders = (owner_index[:, :, :, None] - offsets[:, None, None, :]) % N_SEQ
    sender_key = senders * BLK_DEV + jnp.arange(BLK_DEV, dtype=jnp.int32)[None, None, None, :]
    own_key = source[None, :, None] * BLK_DEV + jnp.arange(BLK_DEV, dtype=jnp.int32)[None, None, :]
    rank_order = jnp.sum((sender_key < own_key[..., None]).astype(jnp.int32), axis=-1)
    position = (owner_index * BLK_DEV + rank_order).reshape(H, TOTAL_BLOCKS)
    head_rows = jnp.arange(H, dtype=jnp.int32)[:, None]
    block_ids = jnp.broadcast_to(jnp.arange(TOTAL_BLOCKS, dtype=jnp.int32)[None, :], (H, TOTAL_BLOCKS))
    sorted_block = jnp.zeros((H, TOTAL_BLOCKS), jnp.int32).at[head_rows, position].set(block_ids)
    forced = jnp.concatenate([jnp.zeros((H, 1), bool), sorted_block[:, 1:] < sorted_block[:, :-1]], axis=1)
    scoring_keys = jax.random.split(jax.random.fold_in(key, 12), H)
    score_matrix = jax.vmap(lambda sorted_key: jax.random.permutation(sorted_key, TOTAL_BLOCKS))(scoring_keys).astype(jnp.int32)
    score_matrix = jnp.where(forced, score_matrix + TOTAL_BLOCKS, score_matrix)
    score_matrix = score_matrix.at[:, 0].set(-1)
    picked = lax.top_k(score_matrix, NBUCK - 1)[1].astype(jnp.int32)
    breaks = jnp.zeros((H, TOTAL_BLOCKS), jnp.int32).at[head_rows, picked].set(1)
    labels = jnp.cumsum(breaks, axis=1).astype(jnp.int32)
    bucket_ids = jnp.take_along_axis(labels, position, axis=1)
    return jnp.transpose(bucket_ids).astype(jnp.int32)


def shard_levels(key, extent, cuts, low, top_value):
    level, own = 1.0, jax.random.fold_in(key, 6)
    for axis_at, blocks in cuts:
        heights = jnp.exp(jax.random.uniform(jax.random.fold_in(own, axis_at), (blocks,), jnp.float32, low / len(cuts), top_value / len(cuts)))
        level = level * jnp.repeat(heights, extent[axis_at] // blocks).reshape([-1 if axis == axis_at else 1 for axis in range(len(extent))])
    return level


def centred(key, shape, spread, limit, cuts=(), held_as=jnp.bfloat16):
    factor_of = shard_levels(key, shape, cuts, -0.22, 0.18) if cuts else 1.0
    drawn = jax.random.normal(key, shape, jnp.float32) * spread * factor_of
    return jnp.minimum(jnp.maximum(drawn, -limit), limit).astype(held_as)


def setup_inputs(seed: int = 0) -> dict:
    key_of = jax.random.split(jax.random.key(seed), 6)
    tokens = draw_tokens(jax.random.fold_in(key_of[5], 71), 0)
    buckets = draw_buckets(jax.random.fold_in(key_of[5], 71), 0)
    w_shared = draw_w_shared(jax.random.fold_in(key_of[5], 71), 0)
    w_value = centred(key_of[3], (D, D), D ** -0.5, 0.1875, ((1, 4),))
    w_output = centred(key_of[4], (D, D), D ** -0.5, 0.1875, ((1, 4),))
    return dict(tokens=tokens, buckets=buckets, w_shared=w_shared, w_value=w_value, w_output=w_output)


def attend(sorted_shared, value_sorted):
    preceding_s = jnp.roll(sorted_shared, 1, axis=0)
    preceding_v = jnp.roll(value_sorted, 1, axis=0)
    key_shared = jnp.concatenate([preceding_s, sorted_shared], axis=1)
    key_values = jnp.concatenate([preceding_v, value_sorted], axis=1)
    key_float = key_shared.astype(jnp.float32)
    khat = (key_float * lax.rsqrt(lax.optimization_barrier(jnp.mean(key_float * key_float, axis=-1, keepdims=True)) + 1e-06)).astype(jnp.bfloat16)
    scores = jnp.einsum('nqd,nkd->nqk', sorted_shared.astype(jnp.float32), khat.astype(jnp.float32)) * DH ** (-0.5)
    self_mask = jnp.arange(2 * BLK)[None, :] == jnp.arange(BLK)[:, None] + BLK
    scores = jnp.where(self_mask[None], jnp.float32(-100000.0), scores)
    row_max = lax.optimization_barrier(jnp.max(scores, axis=-1, keepdims=True))
    expo = jnp.exp(scores - row_max)
    weights = (expo / lax.optimization_barrier(jnp.sum(expo, axis=-1, keepdims=True))).astype(jnp.bfloat16)
    return jnp.einsum('nqk,nkd->nqd', weights.astype(jnp.float32), key_values.astype(jnp.float32)).astype(jnp.bfloat16)

def reference(tokens, buckets, w_shared, w_value, w_output):

    def one_head(head_id):
        start = (head_id * DH).astype(jnp.int32)
        head_cols = lax.dynamic_slice_in_dim(w_shared, start, DH, 1)
        value_cols = lax.dynamic_slice_in_dim(w_value, start, DH, 1)
        shared = jnp.dot(tokens, head_cols, preferred_element_type=jnp.float32).astype(jnp.bfloat16)
        values = jnp.dot(tokens, value_cols, preferred_element_type=jnp.float32).astype(jnp.bfloat16)
        ordering = jnp.argsort(jnp.take(buckets, head_id, axis=1), stable=True).astype(jnp.int32)
        sorted_shared = shared.reshape(TOTAL_BLOCKS, BLK, DH)[ordering]
        value_sorted = values.reshape(TOTAL_BLOCKS, BLK, DH)[ordering]
        result = attend(sorted_shared, value_sorted)
        placed = jnp.zeros_like(result).at[ordering].set(result)
        return placed.reshape(TOKENS, DH)
    per_head = lax.map(one_head, jnp.arange(H, dtype=jnp.int32))
    attention = jnp.transpose(per_head, (1, 0, 2)).reshape(TOKENS, D)
    mixed = tokens.astype(jnp.float32) + jnp.dot(attention, w_output, preferred_element_type=jnp.float32)
    return mixed.astype(jnp.bfloat16)
```

```python
import functools

import jax
import jax.numpy as jnp
from jax import lax
from jax.experimental import pallas as pl
from jax.experimental.pallas import tpu as pltpu
from jax.sharding import PartitionSpec as P

DH = 64
BLK = 128
HG = 4
LANES = 128
PARTS = 4
ROWS = BLK // PARTS
FOLD = ROWS // 2
HALVES = 2
HROWS = BLK // HALVES
HFOLD = HROWS // 2
MESH = pl.DeviceIdType.MESH


def head_ring():
    g = lax.axis_index("head")
    h1 = g + 1 - 2 * lax.rem(g, 2)
    h2 = g + 2 - 4 * lax.div(g, 2)
    h3 = h1 + 2 - 4 * lax.div(h1, 2)
    return g, h1, h2, h3


def remote(src, dst, send, recv, seq, head):
    return pltpu.make_async_remote_copy(
        src_ref=src, dst_ref=dst, send_sem=send, recv_sem=recv,
        device_id=(seq, head), device_id_type=MESH,
    )


def greet(n, i, g, siblings):
    barrier = pltpu.get_barrier_semaphore()

    def say(p, c):
        pl.semaphore_signal(barrier, inc=1, device_id=(lax.rem(i + p, n), g), device_id_type=MESH)
        return c

    lax.fori_loop(1, n, say, 0)
    for h in siblings:
        pl.semaphore_signal(barrier, inc=1, device_id=(i, h), device_id_type=MESH)
    pl.semaphore_wait(barrier, n + 2)


def rows_of(*parts):
    rows = list(parts)
    rows += [jnp.zeros_like(rows[0])] * (8 - len(rows))
    return jnp.concatenate(rows, axis=0)


def column_of(row):
    return jnp.transpose(jnp.broadcast_to(row, (LANES, LANES)))


def down(x):
    return jnp.sum(x, axis=0, keepdims=True)


def tables(n, nb, cap, i, ids, key_col, place_col, pos_row, target_row, tab):
    blocks, slots = n * nb, n * cap
    tiles = blocks // LANES
    per = LANES // nb
    lane = lax.broadcasted_iota(jnp.int32, (1, LANES), 1)
    across = lax.broadcasted_iota(jnp.int32, (LANES, LANES), 1)
    along = lax.broadcasted_iota(jnp.int32, (LANES, LANES), 0)
    earlier = along < across
    zero = jnp.zeros((1, LANES), jnp.int32)

    def keys(q, carry):
        total = ids[q * per]
        for o in range(1, per):
            total = total + ids[q * per + o]
        key = total * blocks + (q * LANES + lane)
        pos_row[q] = key
        for h in range(HG):
            key_col[q, h] = column_of(key[h:h + 1])
        return carry

    lax.fori_loop(0, tiles, keys, 0)

    def ranks(q, carry):
        key = pos_row[q]
        ranked = []
        for h in range(HG):
            def below(t, acc):
                return acc + down((key_col[t, h] < key[h:h + 1]).astype(jnp.int32))
            ranked.append(lax.fori_loop(0, tiles, below, zero))
        pos_row[q] = rows_of(*ranked)
        return carry

    lax.fori_loop(0, tiles, ranks, 0)

    def places(q, carry):
        inverse, code_at = carry
        pos = pos_row[q]
        owner = pos // nb
        src = (q * LANES + lane) // nb
        src_col = (q * LANES + along) // nb
        pair = owner + n * src
        pos_cols = [column_of(pos[h:h + 1]) for h in range(HG)]
        pair_cols = [p // nb + n * src_col for p in pos_cols]
        ks = []
        for h in range(HG):
            mine = pair[h:h + 1]
            k = down(((pair_cols[h] == mine) & earlier).astype(jnp.int32))
            for o in range(h):
                k = k + down((pair_cols[o] == mine).astype(jnp.int32))
            ks.append(k)
            k_col = column_of(k)
            place = jnp.where(pos_cols[h] // nb == i, src_col * cap + k_col, -1)
            code = pos_cols[h] + h * blocks
            place_col[q, h] = place
            key_col[q, h] = code
            code_at = code_at + down(jnp.where(place == across, code, 0))
            target = jnp.where(src_col == i, (pos_cols[h] // nb) * cap + k_col, -1)
            item = (along % nb) * HG + h
            inverse = inverse + down(jnp.where(target == across, item, 0))
        target_row[q] = jnp.minimum(owner * cap + rows_of(*ks), slots - 1)
        return inverse, code_at

    inverse, code_at = lax.fori_loop(0, tiles, places, (zero, zero))
    last_at = lane * blocks + i * nb + nb - 1

    def links(q, carry):
        before, tails = carry
        for h in range(HG):
            place, code = place_col[q, h], key_col[q, h]
            before = before + down(jnp.where((code == code_at - 1) & (place >= 0), place, 0))
            tails = tails + down(jnp.where((code == last_at) & (place >= 0), place, 0))
        return before, tails

    before, tails = lax.fori_loop(0, tiles, links, (zero, zero))
    before = jnp.where(code_at % nb == 0, slots + code_at // blocks, before)
    tab[...] = rows_of(jnp.minimum(inverse, nb * HG - 1), jnp.clip(before, 0, slots + HG - 1),
                       jnp.minimum(tails, slots - 1))


def main_kernel(n, cap, nb, buck_hbm, tok, ws_hbm, wv_hbm, wo_hbm, out,
                buck, sent, ids, key_col, place_col, pos_row, target_row, tab, idx, targets, goals,
                own, ws, wv, wo, g1, g2, g3, items_s, items_v, s_out, v_out, s_in, v_in,
                ts_out, ts_in, tv_out, tv_in, qbuf, kbuf, vbuf, wbuf, out2, ans0, ans1,
                local, wload, sb, rb, sg, rg, sx, rx, sc, rc, so, ro, ss, rs, sv, rv, st, rt,
                sr, rr, s1, r1, s2, r2, s3, r3):
    ans = (ans0, ans1)
    i = lax.axis_index("seq")
    g, h1, h2, h3 = head_ring()
    width = tok.shape[-1]
    slots = n * cap

    def part_of(c):
        return tok.at[:, pl.ds(c * ROWS, ROWS), :]

    loads = [pltpu.make_async_copy(src, dst, wload.at[k])
             for k, (src, dst) in enumerate(((ws_hbm, ws), (wv_hbm, wv), (wo_hbm, wo)))]
    own_loads = [pltpu.make_async_copy(part_of(c), own.at[c], local.at[c]) for c in range(PARTS)]
    fetch = pltpu.make_async_copy(buck_hbm, buck, wload.at[3])
    fetch.start()
    loads[0].start()
    for load in own_loads:
        load.start()
    loads[1].start()
    loads[2].start()
    per = LANES // nb
    sent[...] = jnp.zeros_like(sent)
    fetch.wait()
    sent[:HG, :nb] = buck[...]
    sent[...] = pltpu.roll(sent[...], lax.rem(i, per) * nb, 1)
    ids[i] = sent[...]
    greet(n, i, g, (h1, h2, h3))

    def bucket_copy(p):
        peer = lax.rem(i + p, n)
        return remote(sent, ids.at[i], sb.at[peer], rb.at[i], peer, g)

    def bucket_start(p, carry):
        bucket_copy(p).start()
        return carry

    lax.fori_loop(1, n, bucket_start, 0)

    def over_x(c):
        return remote(part_of(c), g2.at[c], sx.at[c], rx.at[c], i, h2)

    def over_core(c):
        return remote(part_of(c), g1.at[c], sc.at[c], rc.at[c], i, h1)

    def onward(c):
        return remote(g2.at[c], g3.at[c], so.at[c], ro.at[c], i, h1)

    for c in range(PARTS):
        over_x(c).start()
        over_core(c).start()

    def bucket_wait(p, carry):
        src = lax.rem(i + n - p, n)
        remote(sent, ids.at[src], sb.at[src], rb.at[src], src, g).wait_recv()
        return carry

    lax.fori_loop(1, n, bucket_wait, 0)
    tables(n, nb, cap, i, ids, key_col, place_col, pos_row, target_row, tab)
    to_scalar = pltpu.make_async_copy(tab, idx, wload.at[3])
    to_scalar.start()
    targets[0] = target_row[lax.div(i, per)]
    goal_copies = [remote(targets.at[0], targets.at[r], sg.at[r], rg.at[r], i, h)
                   for r, h in ((1, h1), (2, h2), (3, h3))]
    for copy in goal_copies:
        copy.start()
    for load in loads:
        load.wait()
    for load in own_loads:
        load.wait()
    to_scalar.wait()

    def chunk(o):
        return pl.ds(o * cap, cap)

    def send_s(c, p):
        peer = lax.rem(i + p, n)
        return remote(s_out.at[c, peer], s_in.at[c, chunk(i)], ss.at[c, peer], rs.at[c, i], peer, g)

    def send_v(p):
        peer = lax.rem(i + p, n)
        return remote(v_out.at[peer], v_in.at[chunk(i)], sv.at[peer], rv.at[i], peer, g)

    low = lax.broadcasted_iota(jnp.int32, (FOLD, 2 * DH), 1) < DH
    low_v = lax.broadcasted_iota(jnp.int32, (BLK // 2, 2 * DH), 1) < DH
    low_h = lax.broadcasted_iota(jnp.int32, (HFOLD, 2 * DH), 1) < DH
    query_scale = jnp.where(lax.broadcasted_iota(jnp.int32, (1, 2 * DH), 1) < DH,
                            jnp.float32(DH ** -0.5), jnp.float32(0.0))

    def unfold(x):
        x = x.astype(jnp.float32)
        turned = pltpu.roll(x, DH, 1)
        return jnp.concatenate([jnp.where(low, x, turned), jnp.where(low, turned, x)], axis=0)

    def khat_of(x):
        square = jnp.sum(x * x, axis=1, keepdims=True) * (0.5 / DH)
        return (x * lax.rsqrt(square + 1e-6)).astype(jnp.bfloat16)

    step_blocks = min(nb, 8)

    def project(c, w, items):
        def one(q, carry):
            total = jnp.zeros((step_blocks * ROWS, HG * DH), jnp.float32)
            for ref, h in ((own, g), (g1, h1), (g2, h2), (g3, h3)):
                x = ref[c, pl.ds(q * step_blocks, step_blocks)].reshape(step_blocks * ROWS, width)
                total += jnp.dot(x, w[pl.ds(pl.multiple_of(h * width, width), width), :],
                                 preferred_element_type=jnp.float32)
            full = total.astype(jnp.bfloat16)
            for b in range(step_blocks):
                for h in range(HG):
                    cols = slice(h * DH, (h + 1) * DH)
                    items[c, (q * step_blocks + b) * HG + h] = jnp.concatenate(
                        [full[b * ROWS: b * ROWS + FOLD, cols],
                         full[b * ROWS + FOLD: (b + 1) * ROWS, cols]], axis=1)
            return carry

        lax.fori_loop(0, nb // step_blocks, one, 0)

    def ready_s(c, o):
        rows = pl.ds(pl.multiple_of(c * ROWS, ROWS), ROWS)
        for k in range(cap):
            j = o * cap + k
            x = unfold(s_in[c, j])
            qbuf[j, rows] = (x * query_scale).astype(jnp.bfloat16)
            kbuf[j, rows] = khat_of(x)

    def arrive_s(c):
        ready_s(c, i)

        def one(p, carry):
            src = lax.rem(i + n - p, n)
            remote(s_out.at[c, src], s_in.at[c, chunk(src)], ss.at[c, src], rs.at[c, src], src, g).wait_recv()
            ready_s(c, src)
            return carry

        lax.fori_loop(1, n, one, 0)

    def gather(c, carry):
        over_x(c).wait_recv()
        onward(c).start()
        over_core(c).wait_recv()
        onward(c).wait_recv()
        project(c, ws, items_s)

        def pack(p, carry):
            peer = lax.rem(i + p, n)
            for k in range(cap):
                s_out[c, peer, k] = items_s[c, idx[0, peer * cap + k]]
            send_s(c, p).start()
            return carry

        lax.fori_loop(1, n, pack, 0)
        for k in range(cap):
            s_in[c, i * cap + k] = items_s[c, idx[0, i * cap + k]]
        project(c, wv, items_v)

        @pl.when(c > 0)
        def _():
            arrive_s(c - 1)
        return carry

    lax.fori_loop(0, PARTS, gather, 0)

    def pack_v(p, carry):
        peer = lax.rem(i + p, n)
        for k in range(cap):
            at = idx[0, peer * cap + k]
            for c in range(PARTS):
                v_out[peer, k, c * FOLD:(c + 1) * FOLD] = items_v[c, at]
        send_v(p).start()
        return carry

    lax.fori_loop(1, n, pack_v, 0)
    for k in range(cap):
        at = idx[0, i * cap + k]
        for c in range(PARTS):
            v_in[i * cap + k, c * FOLD:(c + 1) * FOLD] = items_v[c, at]
    arrive_s(PARTS - 1)

    for h in range(HG):
        at = idx[2, h]
        for c in range(PARTS):
            ts_out[h, c] = s_in[c, at]
    following = lax.rem(i + 1, n)
    tail_s = remote(ts_out, ts_in, st.at[0], rt.at[0], following, g)
    tail_s.start()

    def ready_v_from(x):
        return jnp.concatenate([unfold(x[c * FOLD:(c + 1) * FOLD]) for c in range(PARTS)],
                               axis=0).astype(jnp.bfloat16)

    def ready_v(o):
        for k in range(cap):
            j = o * cap + k
            vbuf[j] = ready_v_from(v_in[j])

    ready_v(i)
    tail_s.wait_recv()
    for h in range(HG):
        for c in range(PARTS):
            kbuf[slots + h, c * ROWS:(c + 1) * ROWS] = khat_of(unfold(ts_in[h, c]))

    row_at = lax.broadcasted_iota(jnp.int32, (BLK, 2 * BLK), 0)
    col_at = lax.broadcasted_iota(jnp.int32, (BLK, 2 * BLK), 1)
    itself = col_at == row_at + BLK

    def weigh(o, carry):
        for k in range(cap):
            j = o * cap + k
            keys = jnp.concatenate([kbuf[idx[1, j]], kbuf[j]], axis=0)
            scores = lax.dot_general(qbuf[j], keys, (((1,), (1,)), ((), ())),
                                     preferred_element_type=jnp.float32)
            scores = jnp.where(itself, jnp.float32(-100000.0), scores)
            expo = jnp.exp(scores - jnp.max(scores, axis=1, keepdims=True))
            wbuf[j] = (expo * (1.0 / jnp.sum(expo, axis=1, keepdims=True))).astype(jnp.bfloat16)
        return carry

    lax.fori_loop(0, n, weigh, 0)
    for copy in goal_copies:
        copy.wait_recv()
    goal_scalar = pltpu.make_async_copy(targets, goals, wload.at[3])
    goal_scalar.start()

    def arrive_v(p, carry):
        src = lax.rem(i + n - p, n)
        remote(v_out.at[src], v_in.at[chunk(src)], sv.at[src], rv.at[src], src, g).wait_recv()
        ready_v(src)
        return carry

    lax.fori_loop(1, n, arrive_v, 0)
    for h in range(HG):
        tv_out[h] = v_in[idx[2, h]]
    tail_v = remote(tv_out, tv_in, st.at[1], rt.at[1], following, g)
    tail_v.start()
    tail_v.wait_recv()
    for h in range(HG):
        vbuf[slots + h] = ready_v_from(tv_in[h])

    def attend(q, j):
        values = jnp.concatenate([vbuf[idx[1, j]], vbuf[j]], axis=0)
        rows = pl.ds(pl.multiple_of(q * HROWS, HROWS), HROWS)
        mixed = jnp.dot(wbuf[j, rows], values, preferred_element_type=jnp.float32)
        return jnp.where(low_h, mixed[:HFOLD], mixed[HFOLD:]).astype(jnp.bfloat16)

    def reply(q, p):
        peer = lax.rem(i + p, n)
        return remote(out2.at[q, peer], ans[q].at[0, chunk(i)], sr.at[q, peer], rr.at[q, i], peer, g)

    def relay1(q, o):
        return remote(ans[q].at[0, chunk(o)], ans[q].at[1, chunk(o)], s1.at[q, o], r1.at[q, o], i, h1)

    def relay2(q, o):
        return remote(ans[q].at[0, chunk(o)], ans[q].at[2, chunk(o)], s2.at[q, o], r2.at[q, o], i, h2)

    def relay3(q, o):
        return remote(ans[q].at[2, chunk(o)], ans[q].at[3, chunk(o)], s3.at[q, o], r3.at[q, o], i, h1)

    def stride(t):
        odd = lax.rem(t, 2)
        return (1 - odd) * (lax.div(t, 2) + 1) + odd * (n - lax.div(t + 1, 2))

    steps = n - 1

    def answer(q, t):
        p = stride(t)
        peer = lax.rem(i + p, n)
        for k in range(cap):
            out2[q, peer, k] = attend(q, peer * cap + k)
        reply(q, p).start()

    def relay(q, t):
        src = lax.rem(i + n - stride(t), n)
        remote(out2.at[q, src], ans[q].at[0, chunk(src)], sr.at[q, src], rr.at[q, src], src, g).wait_recv()
        relay2(q, src).start()
        relay1(q, src).start()

    def spread(q, t):
        src = lax.rem(i + n - stride(t), n)
        relay2(q, src).wait_recv()
        relay3(q, src).start()

    def own_answer(q):
        for k in range(cap):
            ans[q][0, i * cap + k] = attend(q, i * cap + k)
        relay2(q, i).start()
        relay1(q, i).start()

    def settle(q):
        def one(o, carry):
            relay1(q, o).wait_recv()
            relay3(q, o).wait_recv()
            return carry

        lax.fori_loop(0, n, one, 0)

    goal_scalar.wait()
    group = 4

    def finish(half):
        def one(q, carry):
            total = jnp.zeros((group * HROWS, width), jnp.float32)
            for r, h in enumerate((g, h1, h2, h3)):
                rows = []
                for b in range(group):
                    at = lax.rem(i, per) * nb + q * group + b
                    parts = [ans[half][r, goals[r, k, at]] for k in range(HG)]
                    rows.append(jnp.concatenate([x[:, :DH] for x in parts], axis=1))
                    rows.append(jnp.concatenate([x[:, DH:] for x in parts], axis=1))
                total += jnp.dot(jnp.concatenate(rows, axis=0),
                                 wo[pl.ds(pl.multiple_of(h * HG * DH, HG * DH), HG * DH), :],
                                 preferred_element_type=jnp.float32)
            at = pl.ds(q * group, group)
            total = total.reshape(group, HROWS, width)
            inner = HROWS // ROWS
            for c in range(inner):
                base = own[half * inner + c, at].astype(jnp.float32)
                out[at, half * HROWS + c * ROWS: half * HROWS + (c + 1) * ROWS] = (
                    base + total[:, c * ROWS:(c + 1) * ROWS]).astype(jnp.bfloat16)
            return carry

        lax.fori_loop(0, nb // group, one, 0)

    ahead = 3

    def flow(q):
        def one(t, carry):
            answer(q, t)
            relay(q, t - ahead)

            @pl.when(t > ahead)
            def _():
                spread(q, t - ahead - 1)
            return carry

        lax.fori_loop(ahead, steps, one, 0)

    def begin(q, also):
        for t in range(ahead):
            answer(q, t)
            if t == 0:
                own_answer(q)
            also(t)
        relay2(q, i).wait_recv()
        relay3(q, i).start()

    def ebb(q):
        def one(t, carry):
            relay(q, t)
            spread(q, t - 1)
            return carry

        lax.fori_loop(steps - ahead, steps, one, 0)
        spread(q, steps - 1)

    def over(t):
        relay(0, steps - ahead + t)
        spread(0, steps - ahead + t - 1)

    begin(0, lambda t: None)
    flow(0)
    begin(1, over)
    spread(0, steps - 1)
    flow(1)
    settle(0)
    finish(0)
    ebb(1)
    settle(1)
    finish(1)
    for copy in goal_copies:
        copy.wait_send()

    def drain(p, carry):
        bucket_copy(p).wait_send()
        for c in range(PARTS):
            send_s(c, p).wait_send()
        send_v(p).wait_send()
        for q in range(HALVES):
            reply(q, p).wait_send()
        return carry

    lax.fori_loop(1, n, drain, 0)
    for c in range(PARTS):
        over_x(c).wait_send()
        over_core(c).wait_send()
        onward(c).wait_send()
    tail_s.wait_send()
    tail_v.wait_send()

    def drain_relays(o, carry):
        for q in range(HALVES):
            relay1(q, o).wait_send()
            relay2(q, o).wait_send()
            relay3(q, o).wait_send()
        return carry

    lax.fori_loop(0, n, drain_relays, 0)


def per_device(tokens, buckets, w_shared, w_value, w_output):
    n = lax.axis_size("seq")
    nb = buckets.shape[0]
    rows, width = tokens.shape
    cap = max(1, nb * HG // n)
    slots = n * cap
    bf = jnp.bfloat16
    vmem = pl.BlockSpec(memory_space=pltpu.VMEM)
    tiles = n * nb // LANES
    i32 = jnp.int32
    square = pltpu.VMEM((tiles, HG, LANES, LANES), i32)
    line = pltpu.VMEM((tiles, 8, LANES), i32)
    hbm = pl.BlockSpec(memory_space=pltpu.HBM)
    dma = lambda *k: pltpu.SemaphoreType.DMA(k)
    gathered = pltpu.VMEM((PARTS, nb, ROWS, width), bf)
    weight = pltpu.VMEM(w_shared.shape, bf)
    small = (FOLD, 2 * DH)
    half = (BLK // 2, 2 * DH)
    out = pl.pallas_call(
        functools.partial(main_kernel, n, cap, nb),
        out_shape=jax.ShapeDtypeStruct((nb, BLK, width), bf),
        in_specs=[hbm] * 5,
        out_specs=vmem,
        scratch_shapes=[pltpu.VMEM((HG, nb), i32), pltpu.VMEM((8, LANES), i32), pltpu.VMEM((n, 8, LANES), i32)]
        + [square] * 2 + [line] * 2
        + [pltpu.VMEM((8, LANES), i32), pltpu.SMEM((8, LANES), i32)]
        + [pltpu.VMEM((HG, 8, LANES), i32), pltpu.SMEM((HG, 8, LANES), i32)]
        + [gathered] + [weight] * 3 + [gathered] * 3
        + [pltpu.VMEM((PARTS, nb * HG) + small, bf)] * 2
        + [pltpu.VMEM((PARTS, n, cap) + small, bf), pltpu.VMEM((n, cap) + half, bf)]
        + [pltpu.VMEM((PARTS, slots) + small, bf), pltpu.VMEM((slots,) + half, bf)]
        + [pltpu.VMEM((HG, PARTS) + small, bf)] * 2
        + [pltpu.VMEM((HG,) + half, bf)] * 2
        + [pltpu.VMEM((slots, BLK, 2 * DH), bf)]
        + [pltpu.VMEM((slots + HG, BLK, 2 * DH), bf)] * 2
        + [pltpu.VMEM((slots, BLK, 2 * BLK), bf)]
        + [pltpu.VMEM((HALVES, n, cap, HFOLD, 2 * DH), bf), pltpu.VMEM((HG, slots, HFOLD, 2 * DH), bf)] + [pltpu.VMEM((HG, slots, HFOLD, 2 * DH), bf)]
        + [dma(PARTS), dma(4)] + [dma(n)] * 2 + [dma(HG)] * 2 + [dma(PARTS)] * 6 + [dma(PARTS, n)] * 2 + [dma(n)] * 2 + [dma(2)] * 2
        + [dma(HALVES, n)] * 8,
        compiler_params=pltpu.CompilerParams(collective_id=0, has_side_effects=True,
                                             vmem_limit_bytes=60 << 20),
    )(buckets.T, tokens.reshape(nb, BLK, width), w_shared, w_value, w_output)
    return out.reshape(rows, width)


def solution(mesh):
    return jax.shard_map(
        per_device,
        mesh=mesh,
        in_specs=(
            P("seq", "head"),
            P("seq", "head"),
            P(None, "head"),
            P(None, "head"),
            P(None, "head"),
        ),
        out_specs=P("seq", "head"),
        check_vma=False,
    )
```

```python
import functools

import jax
import jax.numpy as jnp
from jax import lax
from jax.experimental import pallas as pl
from jax.experimental.pallas import tpu as pltpu
from jax.sharding import PartitionSpec as P

DH = 64
BLK = 128
HG = 4
LANES = 128
PARTS = 4
ROWS = BLK // PARTS
FOLD = ROWS // 2
HALVES = 2
DV = DH // HALVES
QUART = 4
QROWS = BLK // QUART
MESH = pl.DeviceIdType.MESH


def head_ring():
    g = lax.axis_index("head")
    h1 = g + 1 - 2 * lax.rem(g, 2)
    h2 = g + 2 - 4 * lax.div(g, 2)
    h3 = h1 + 2 - 4 * lax.div(h1, 2)
    return g, h1, h2, h3


def remote(src, dst, send, recv, seq, head):
    return pltpu.make_async_remote_copy(
        src_ref=src, dst_ref=dst, send_sem=send, recv_sem=recv,
        device_id=(seq, head), device_id_type=MESH,
    )


def greet(n, i, g, siblings):
    barrier = pltpu.get_barrier_semaphore()

    def say(p, c):
        pl.semaphore_signal(barrier, inc=1, device_id=(lax.rem(i + p, n), g), device_id_type=MESH)
        return c

    lax.fori_loop(1, n, say, 0)
    for h in siblings:
        pl.semaphore_signal(barrier, inc=1, device_id=(i, h), device_id_type=MESH)


def greeted(n):
    pl.semaphore_wait(pltpu.get_barrier_semaphore(), n + 2)


def rows_of(*parts):
    rows = list(parts)
    rows += [jnp.zeros_like(rows[0])] * (8 - len(rows))
    return jnp.concatenate(rows, axis=0)


def column_of(row):
    return jnp.transpose(jnp.broadcast_to(row, (LANES, LANES)))


def down(x):
    return jnp.sum(x, axis=0, keepdims=True)


def tables(n, nb, cap, i, ids, key_col, place_col, pos_row, target_row, tab):
    blocks, slots = n * nb, n * cap
    tiles = blocks // LANES
    per = LANES // nb
    lane = lax.broadcasted_iota(jnp.int32, (1, LANES), 1)
    across = lax.broadcasted_iota(jnp.int32, (LANES, LANES), 1)
    along = lax.broadcasted_iota(jnp.int32, (LANES, LANES), 0)
    earlier = along < across
    zero = jnp.zeros((1, LANES), jnp.int32)

    def keys(q, carry):
        total = ids[q * per]
        for o in range(1, per):
            total = total + ids[q * per + o]
        key = total * blocks + (q * LANES + lane)
        pos_row[q] = key
        for h in range(HG):
            key_col[q, h] = column_of(key[h:h + 1])
        return carry

    lax.fori_loop(0, tiles, keys, 0)

    def ranks(q, carry):
        key = pos_row[q]
        ranked = []
        for h in range(HG):
            def below(t, acc):
                return acc + down((key_col[t, h] < key[h:h + 1]).astype(jnp.int32))
            ranked.append(lax.fori_loop(0, tiles, below, zero))
        pos_row[q] = rows_of(*ranked)
        return carry

    lax.fori_loop(0, tiles, ranks, 0)

    def places(q, carry):
        inverse, code_at = carry
        pos = pos_row[q]
        owner = pos // nb
        src = (q * LANES + lane) // nb
        src_col = (q * LANES + along) // nb
        pair = owner + n * src
        pos_cols = [column_of(pos[h:h + 1]) for h in range(HG)]
        pair_cols = [p // nb + n * src_col for p in pos_cols]
        ks = []
        for h in range(HG):
            mine = pair[h:h + 1]
            k = down(((pair_cols[h] == mine) & earlier).astype(jnp.int32))
            for o in range(h):
                k = k + down((pair_cols[o] == mine).astype(jnp.int32))
            ks.append(k)
            k_col = column_of(k)
            place = jnp.where(pos_cols[h] // nb == i, src_col * cap + k_col, -1)
            code = pos_cols[h] + h * blocks
            place_col[q, h] = place
            key_col[q, h] = code
            code_at = code_at + down(jnp.where(place == across, code, 0))
            target = jnp.where(src_col == i, (pos_cols[h] // nb) * cap + k_col, -1)
            item = (along % nb) * HG + h
            inverse = inverse + down(jnp.where(target == across, item, 0))
        target_row[q] = jnp.minimum(owner * cap + rows_of(*ks), slots - 1)
        return inverse, code_at

    inverse, code_at = lax.fori_loop(0, tiles, places, (zero, zero))
    last_at = lane * blocks + i * nb + nb - 1

    def links(q, carry):
        before, tails = carry
        for h in range(HG):
            place, code = place_col[q, h], key_col[q, h]
            before = before + down(jnp.where((code == code_at - 1) & (place >= 0), place, 0))
            tails = tails + down(jnp.where((code == last_at) & (place >= 0), place, 0))
        return before, tails

    before, tails = lax.fori_loop(0, tiles, links, (zero, zero))
    before = jnp.where(code_at % nb == 0, slots + code_at // blocks, before)
    tab[...] = rows_of(jnp.minimum(inverse, nb * HG - 1), jnp.clip(before, 0, slots + HG - 1),
                       jnp.minimum(tails, slots - 1), jnp.clip(code_at // blocks, 0, HG - 1))


def main_kernel(n, cap, nb, buck_hbm, tok, ws_hbm, wv_hbm, wo_hbm, out,
                buck, sent, ids, key_col, place_col, pos_row, target_row, tab, idx, targets, goals,
                own, ws, wv, wo, wo_part, spread_v, g1, g2, g3, items_s, values, items_v, s_out, v_out,
                s_in, v_in0, v_in1, ts_out, ts_in, tv_out, tv_in, qbuf, kbuf, vbuf0, wbuf,
                out2, ans0, ans1, acc,
                local, wload, sg, rg, sx, rx, sc, rc, so, ro, ss, rs, sv, rv, st, rt,
                sr, rr, s1, r1, s2, r2, s3, r3):
    ans, v_in, vbuf = (ans0, ans1), (v_in0, v_in1), (vbuf0, qbuf)
    i = lax.axis_index("seq")
    g, h1, h2, h3 = head_ring()
    width = tok.shape[-1]
    slots = n * cap

    def part_of(c):
        return tok.at[:, pl.ds(c * ROWS, ROWS), :]

    loads = [pltpu.make_async_copy(src, dst, wload.at[k])
             for k, (src, dst) in enumerate(((ws_hbm, ws), (wv_hbm, wv), (wo_hbm, wo)))]
    own_loads = [pltpu.make_async_copy(part_of(c), own.at[c], local.at[c]) for c in range(PARTS)]
    greet(n, i, g, (h1, h2, h3))
    fetch = pltpu.make_async_copy(buck_hbm, buck, wload.at[3])
    fetch.start()
    loads[0].start()
    for load in own_loads:
        load.start()
    loads[1].start()
    loads[2].start()
    per = LANES // nb
    sent[...] = jnp.zeros_like(sent)
    fetch.wait()
    sent[:HG, :nb] = buck[...]
    sent[...] = pltpu.roll(sent[...], lax.rem(i, per) * nb, 1)
    ids[i] = sent[...]
    greeted(n)

    def bucket_copy(p):
        peer = lax.rem(i + p, n)
        return remote(sent, ids.at[i], sr.at[0, peer], rr.at[0, i], peer, g)

    def bucket_start(p, carry):
        bucket_copy(p).start()
        return carry

    lax.fori_loop(1, n, bucket_start, 0)

    def over_x(c):
        return remote(part_of(c), g2.at[c], sx.at[c], rx.at[c], i, h2)

    def over_core(c):
        return remote(part_of(c), g1.at[c], sc.at[c], rc.at[c], i, h1)

    def onward(c):
        return remote(g2.at[c], g3.at[c], so.at[c], ro.at[c], i, h1)

    for c in range(PARTS):
        over_x(c).start()
        over_core(c).start()

    def bucket_wait(p, carry):
        src = lax.rem(i + n - p, n)
        remote(sent, ids.at[src], sr.at[0, src], rr.at[0, src], src, g).wait()
        return carry

    lax.fori_loop(1, n, bucket_wait, 0)
    tables(n, nb, cap, i, ids, key_col, place_col, pos_row, target_row, tab)
    to_scalar = pltpu.make_async_copy(tab, idx, wload.at[3])
    to_scalar.start()
    targets[0] = target_row[lax.div(i, per)]
    goal_copies = [remote(targets.at[0], targets.at[r], sg.at[r], rg.at[r], i, h)
                   for r, h in ((1, h1), (2, h2), (3, h3))]
    for copy in goal_copies:
        copy.start()
    for load in loads:
        load.wait()
    for load in own_loads:
        load.wait()
    to_scalar.wait()

    def chunk(o):
        return pl.ds(o * cap, cap)

    def send_s(c, p):
        peer = lax.rem(i + p, n)
        return remote(s_out.at[c, peer], s_in.at[c, chunk(i)], ss.at[c, peer], rs.at[c, i], peer, g)

    def send_v(q, p):
        peer = lax.rem(i + p, n)
        return remote(v_out.at[q, peer], v_in[q].at[chunk(i)], sv.at[q, peer], rv.at[q, i], peer, g)

    low = lax.broadcasted_iota(jnp.int32, (FOLD, 2 * DH), 1) < DH
    group_at = lax.broadcasted_iota(jnp.int32, (QROWS, QUART * DV), 1) // DV
    query_scale = jnp.where(lax.broadcasted_iota(jnp.int32, (1, 2 * DH), 1) < DH,
                            jnp.float32(DH ** -0.5), jnp.float32(0.0))

    def unfold(x):
        x = x.astype(jnp.float32)
        turned = pltpu.roll(x, DH, 1)
        return jnp.concatenate([jnp.where(low, x, turned), jnp.where(low, turned, x)], axis=0)

    def khat_of(x):
        square = jnp.sum(x * x, axis=1, keepdims=True) * (0.5 / DH)
        return (x * lax.rsqrt(square + 1e-6)).astype(jnp.bfloat16)

    step_blocks = min(nb, 8)

    def project(c, w, store):
        def one(q, carry):
            total = jnp.zeros((step_blocks * ROWS, HG * DH), jnp.float32)
            for ref, h in ((own, g), (g1, h1), (g2, h2), (g3, h3)):
                x = ref[c, pl.ds(q * step_blocks, step_blocks)].reshape(step_blocks * ROWS, width)
                total += jnp.dot(x, w[pl.ds(pl.multiple_of(h * width, width), width), :],
                                 preferred_element_type=jnp.float32)
            store(c, q * step_blocks, total.astype(jnp.bfloat16))
            return carry

        lax.fori_loop(0, nb // step_blocks, one, 0)

    def store_s(c, at, full):
        for b in range(step_blocks):
            for h in range(HG):
                cols = slice(h * DH, (h + 1) * DH)
                items_s[c, (at + b) * HG + h] = jnp.concatenate(
                    [full[b * ROWS: b * ROWS + FOLD, cols],
                     full[b * ROWS + FOLD: (b + 1) * ROWS, cols]], axis=1)

    def store_v(c, at, full):
        values[pl.ds(at, step_blocks), pl.ds(pl.multiple_of(c * ROWS, ROWS), ROWS)] = (
            full.reshape(step_blocks, ROWS, HG * DH))

    def ready_s(c, o):
        rows = pl.ds(pl.multiple_of(c * ROWS, ROWS), ROWS)
        for k in range(cap):
            j = o * cap + k
            x = unfold(s_in[c, j])
            qbuf[j, rows] = (x * query_scale).astype(jnp.bfloat16)
            kbuf[j, rows] = khat_of(x)

    def arrive_s(c):
        ready_s(c, i)

        def one(p, carry):
            src = lax.rem(i + n - p, n)
            remote(s_out.at[c, src], s_in.at[c, chunk(src)], ss.at[c, src], rs.at[c, src], src, g).wait_recv()
            ready_s(c, src)
            return carry

        lax.fori_loop(1, n, one, 0)

    def gather(c, carry):
        over_x(c).wait_recv()
        onward(c).start()
        over_core(c).wait_recv()
        onward(c).wait_recv()
        project(c, ws, store_s)

        def pack(p, carry):
            peer = lax.rem(i + p, n)
            for k in range(cap):
                s_out[c, peer, k] = items_s[c, idx[0, peer * cap + k]]
            send_s(c, p).start()
            return carry

        lax.fori_loop(1, n, pack, 0)
        for k in range(cap):
            s_in[c, i * cap + k] = items_s[c, idx[0, i * cap + k]]
        project(c, wv, store_v)

        @pl.when(c > 0)
        def _():
            arrive_s(c - 1)
        return carry

    lax.fori_loop(0, PARTS, gather, 0)

    def build_v(q):
        def one(b, carry):
            for h in range(HG):
                cols = slice(h * DH + q * DV, h * DH + (q + 1) * DV)
                items_v[q, b * HG + h] = jnp.concatenate(
                    [values[b, t * QROWS:(t + 1) * QROWS, cols] for t in range(QUART)], axis=1)
            return carry

        lax.fori_loop(0, nb, one, 0)

        def pack(p, carry):
            peer = lax.rem(i + p, n)
            for k in range(cap):
                v_out[q, peer, k] = items_v[q, idx[0, peer * cap + k]]
            return carry

        lax.fori_loop(1, n, pack, 0)
        for k in range(cap):
            v_in[q][i * cap + k] = items_v[q, idx[0, i * cap + k]]

    build_v(0)

    def start_v(p, carry):
        send_v(0, p).start()
        return carry

    lax.fori_loop(1, n, start_v, 0)
    arrive_s(PARTS - 1)

    for h in range(HG):
        at = idx[2, h]
        for c in range(PARTS):
            ts_out[h, c] = s_in[c, at]
    following = lax.rem(i + 1, n)
    tail_s = remote(ts_out, ts_in, st.at[0], rt.at[0], following, g)
    tail_s.start()

    build_v(1)
    l_at = lax.broadcasted_iota(jnp.int32, (QUART * DV, QUART * QUART * DV), 0)
    w_at = lax.broadcasted_iota(jnp.int32, (QUART * DV, QUART * QUART * DV), 1)
    spread_v[...] = ((l_at // DV == w_at // (QUART * DV)) & (l_at % DV == w_at % DV)).astype(
        jnp.float32).astype(jnp.bfloat16)

    def ready_v(q, x, at, count):
        wide = jnp.dot(x.reshape(count * QROWS, QUART * DV), spread_v[...],
                       preferred_element_type=jnp.float32).astype(jnp.bfloat16)
        for t in range(QUART):
            vbuf[q][pl.ds(at, count), t * QROWS:(t + 1) * QROWS] = (
                wide[:, t * QUART * DV:(t + 1) * QUART * DV].reshape(count, QROWS, QUART * DV))

    def ready_v_of(q, o):
        ready_v(q, v_in[q][chunk(o)], o * cap, cap)

    ready_v_of(0, i)
    for r, h in enumerate((g, h1, h2, h3)):
        for q in range(HALVES):
            for t in range(QUART):
                for c in range(QUART):
                    src = pl.multiple_of(h * HG * DH, HG * DH) + (c ^ t) * DH + q * DV
                    wo_part[q, t, (r * QUART + c) * DV:(r * QUART + c + 1) * DV] = wo[pl.ds(src, DV), :]
    tail_s.wait_recv()
    for h in range(HG):
        for c in range(PARTS):
            kbuf[slots + h, c * ROWS:(c + 1) * ROWS] = khat_of(unfold(ts_in[h, c]))

    row_at = lax.broadcasted_iota(jnp.int32, (BLK, 2 * BLK), 0)
    col_at = lax.broadcasted_iota(jnp.int32, (BLK, 2 * BLK), 1)
    itself = col_at == row_at + BLK

    def weigh(o, carry):
        for k in range(cap):
            j = o * cap + k
            keys = jnp.concatenate([kbuf[idx[1, j]], kbuf[j]], axis=0)
            scores = lax.dot_general(qbuf[j], keys, (((1,), (1,)), ((), ())),
                                     preferred_element_type=jnp.float32)
            scores = jnp.where(itself, jnp.float32(-100000.0), scores)
            expo = jnp.exp(scores - jnp.max(scores, axis=1, keepdims=True))
            wbuf[j] = (expo * (1.0 / jnp.sum(expo, axis=1, keepdims=True))).astype(jnp.bfloat16)
        return carry

    lax.fori_loop(0, n, weigh, 0)
    for copy in goal_copies:
        copy.wait_recv()
    goal_scalar = pltpu.make_async_copy(targets, goals, wload.at[3])
    goal_scalar.start()

    def take_v(q, src):
        remote(v_out.at[q, src], v_in[q].at[chunk(src)], sv.at[q, src], rv.at[q, src], src, g).wait_recv()

    def pass_tail(q):
        for h in range(HG):
            tv_out[q, h] = v_in[q][idx[2, h]]
        tail_v(q).start()
        tail_v(q).wait_recv()
        ready_v(q, tv_in[q], slots, HG)

    def tail_v(q):
        return remote(tv_out.at[q], tv_in.at[q], st.at[1 + q], rt.at[1 + q], following, g)

    def attend(q, j):
        keyed = jnp.concatenate([vbuf[q][idx[1, j]], vbuf[q][j]], axis=0)
        mixed = jnp.dot(wbuf[j], keyed, preferred_element_type=jnp.float32)
        turn = group_at ^ idx[3, j]
        picked = mixed[(QUART - 1) * QROWS:]
        for t in range(QUART - 1):
            picked = jnp.where(turn == t, mixed[t * QROWS:(t + 1) * QROWS], picked)
        return picked.astype(jnp.bfloat16)

    pieces = [(0, 0, QROWS), (1, 0, QROWS // 2), (1, QROWS // 2, QROWS // 2)]
    if sr.shape[0] == HALVES:
        pieces = [(0, 0, QROWS), (1, 0, QROWS)]

    def answers_of(e, r, o):
        q, at, count = pieces[e]
        return ans[q].at[r, chunk(o), pl.ds(at, count)]

    def reply_from(e, peer):
        q, at, count = pieces[e]
        return out2.at[q, peer, :, pl.ds(at, count)]

    def reply(e, p):
        peer = lax.rem(i + p, n)
        return remote(reply_from(e, peer), answers_of(e, 0, i), sr.at[e, peer], rr.at[e, i], peer, g)

    def relay1(e, o):
        return remote(answers_of(e, 0, o), answers_of(e, 1, o), s1.at[e, o], r1.at[e, o], i, h1)

    def relay2(e, o):
        return remote(answers_of(e, 0, o), answers_of(e, 2, o), s2.at[e, o], r2.at[e, o], i, h2)

    def relay3(e, o):
        return remote(answers_of(e, 2, o), answers_of(e, 3, o), s3.at[e, o], r3.at[e, o], i, h1)

    def source(p):
        return lax.rem(i + n - p, n)

    def answer(q, p):
        peer = lax.rem(i + p, n)
        for k in range(cap):
            out2[q, peer, k] = attend(q, peer * cap + k)
        reply(q, p).start()

    def relay(e, p):
        src = source(p)
        remote(reply_from(e, src), answers_of(e, 0, src), sr.at[e, src], rr.at[e, src], src, g).wait_recv()
        relay2(e, src).start()
        relay1(e, src).start()

    def spread(e, p):
        relay2(e, source(p)).wait_recv()
        relay3(e, source(p)).start()

    def own_answer(q):
        for k in range(cap):
            ans[q][0, i * cap + k] = attend(q, i * cap + k)
        for e in range(len(pieces)):
            if pieces[e][0] == q:
                relay2(e, i).start()
                relay1(e, i).start()

    def settle(e):
        def one(o, carry):
            relay1(e, o).wait_recv()
            relay3(e, o).wait_recv()
            return carry

        lax.fori_loop(0, n, one, 0)

    goal_scalar.wait()
    mixing = (g1, g3)

    def finish(q):
        def assemble(b, carry):
            for r in range(HG):
                parts = [ans[q][r, goals[r, k, lax.rem(i, per) * nb + b]] for k in range(HG)]
                cols = slice((r % 2) * QUART * DV, (r % 2 + 1) * QUART * DV)
                for t in range(QUART):
                    tile = parts[(QUART - 1) ^ t]
                    for c in range(QUART - 1):
                        tile = jnp.where(group_at == c, parts[c ^ t], tile)
                    mixing[r // 2][t, b, :, cols] = tile
            return carry

        lax.fori_loop(0, nb, assemble, 0)
        depth = 2 * QUART * DV
        for t in range(QUART):
            total = jnp.zeros((nb * QROWS, width), jnp.float32)
            for c in range(HG // 2):
                total += jnp.dot(mixing[c][t].reshape(nb * QROWS, depth), wo_part[q, t, c * depth:(c + 1) * depth],
                                 preferred_element_type=jnp.float32)
            if q == 0:
                acc[t] = own[t].reshape(nb * QROWS, width).astype(jnp.float32) + total
            else:
                out[:, t * QROWS:(t + 1) * QROWS] = (acc[t] + total).astype(jnp.bfloat16).reshape(nb, QROWS, width)

    def each(body, first=1):
        def one(p, carry):
            body(p)
            return carry

        lax.fori_loop(first, n, one, 0)

    def first_values(p):
        take_v(0, source(p))
        send_v(1, p).start()
        ready_v_of(0, source(p))

    def second_values(p):
        take_v(1, source(p))
        ready_v_of(1, source(p))
        relay(0, p)

    each(first_values)
    pass_tail(0)
    own_answer(0)
    each(lambda p: answer(0, p))
    ready_v_of(1, i)
    each(second_values)
    pass_tail(1)
    own_answer(1)
    each(lambda p: answer(1, p))
    spread(0, 0)

    def turn_over(p):
        spread(0, p)
        if len(pieces) > 2:
            reply(1, p).wait_send()
            reply(2, p).start()
        relay(1, p)

    each(turn_over)
    settle(0)
    finish(0)
    if len(pieces) > 2:
        spread(1, 0)

        def last_turn(p):
            spread(1, p)
            relay(2, p)

        each(last_turn)
    each(lambda p: spread(len(pieces) - 1, p), 0)
    for e in range(1, len(pieces)):
        settle(e)
    finish(1)
    for copy in goal_copies:
        copy.wait_send()

    def drain(p, carry):
        for c in range(PARTS):
            send_s(c, p).wait_send()
        for q in range(HALVES):
            send_v(q, p).wait_send()
        reply(0, p).wait_send()
        reply(len(pieces) - 1, p).wait_send()
        return carry

    lax.fori_loop(1, n, drain, 0)
    for c in range(PARTS):
        over_x(c).wait_send()
        over_core(c).wait_send()
        onward(c).wait_send()
    tail_s.wait_send()
    for q in range(HALVES):
        tail_v(q).wait_send()

    def drain_relays(o, carry):
        for e in range(len(pieces)):
            relay1(e, o).wait_send()
            relay2(e, o).wait_send()
            relay3(e, o).wait_send()
        return carry

    lax.fori_loop(0, n, drain_relays, 0)


def per_device(tokens, buckets, w_shared, w_value, w_output):
    n = lax.axis_size("seq")
    nb = buckets.shape[0]
    rows, width = tokens.shape
    cap = max(1, nb * HG // n)
    slots = n * cap
    bf = jnp.bfloat16
    vmem = pl.BlockSpec(memory_space=pltpu.VMEM)
    tiles = n * nb // LANES
    i32 = jnp.int32
    square = pltpu.VMEM((tiles, HG, LANES, LANES), i32)
    line = pltpu.VMEM((tiles, 8, LANES), i32)
    hbm = pl.BlockSpec(memory_space=pltpu.HBM)
    dma = lambda *k: pltpu.SemaphoreType.DMA(k)
    gathered = pltpu.VMEM((PARTS, nb, ROWS, width), bf)
    weight = pltpu.VMEM(w_shared.shape, bf)
    small = (FOLD, 2 * DH)
    quarter = (QROWS, QUART * DV)
    out = pl.pallas_call(
        functools.partial(main_kernel, n, cap, nb),
        out_shape=jax.ShapeDtypeStruct((nb, BLK, width), bf),
        in_specs=[hbm] * 5,
        out_specs=vmem,
        scratch_shapes=[pltpu.VMEM((HG, nb), i32), pltpu.VMEM((8, LANES), i32), pltpu.VMEM((n, 8, LANES), i32)]
        + [square] * 2 + [line] * 2
        + [pltpu.VMEM((8, LANES), i32), pltpu.SMEM((8, LANES), i32)]
        + [pltpu.VMEM((HG, 8, LANES), i32), pltpu.SMEM((HG, 8, LANES), i32)]
        + [gathered] + [weight] * 3
        + [pltpu.VMEM((HALVES, QUART, HG * QUART * DV, width), bf), pltpu.VMEM((QUART * DV, QUART * QUART * DV), bf)]
        + [gathered] * 3
        + [pltpu.VMEM((PARTS, nb * HG) + small, bf), pltpu.VMEM((nb, BLK, HG * DH), bf)]
        + [pltpu.VMEM((HALVES, nb * HG) + quarter, bf)]
        + [pltpu.VMEM((PARTS, n, cap) + small, bf), pltpu.VMEM((HALVES, n, cap) + quarter, bf)]
        + [pltpu.VMEM((PARTS, slots) + small, bf)] + [pltpu.VMEM((slots,) + quarter, bf)] * 2
        + [pltpu.VMEM((HG, PARTS) + small, bf)] * 2
        + [pltpu.VMEM((HALVES, HG) + quarter, bf)] * 2
        + [pltpu.VMEM((slots + HG, BLK, 2 * DH), bf)] * 3
        + [pltpu.VMEM((slots, BLK, 2 * BLK), bf)]
        + [pltpu.VMEM((HALVES, n, cap) + quarter, bf)] + [pltpu.VMEM((HG, slots) + quarter, bf)] * 2
        + [pltpu.VMEM((QUART, nb * QROWS, width), jnp.float32)]
        + [dma(PARTS), dma(4)] + [dma(HG)] * 2 + [dma(PARTS)] * 6 + [dma(PARTS, n)] * 2 + [dma(HALVES, n)] * 2 + [dma(1 + HALVES)] * 2
        + [dma(3 if n <= 16 else HALVES, n)] * 8,
        compiler_params=pltpu.CompilerParams(collective_id=0, has_side_effects=True,
                                             vmem_limit_bytes=62 << 20),
    )(buckets.T, tokens.reshape(nb, BLK, width), w_shared, w_value, w_output)
    return out.reshape(rows, width)


def solution(mesh):
    return jax.shard_map(
        per_device,
        mesh=mesh,
        in_specs=(
            P("seq", "head"),
            P("seq", "head"),
            P(None, "head"),
            P(None, "head"),
            P(None, "head"),
        ),
        out_specs=P("seq", "head"),
        check_vma=False,
    )
```

```python
import functools

import jax
import jax.numpy as jnp
from jax import lax
from jax.experimental import pallas as pl
from jax.experimental.pallas import tpu as pltpu
from jax.sharding import PartitionSpec as P

DH = 64
BLK = 128
HG = 4
LANES = 128
PARTS = 4
ROWS = BLK // PARTS
FOLD = ROWS // 2
HALVES = 2
DV = DH // HALVES
QUART = 4
QROWS = BLK // QUART
MESH = pl.DeviceIdType.MESH


def head_ring():
    g = lax.axis_index("head")
    h1 = g + 1 - 2 * lax.rem(g, 2)
    h2 = g + 2 - 4 * lax.div(g, 2)
    h3 = h1 + 2 - 4 * lax.div(h1, 2)
    return g, h1, h2, h3


def remote(src, dst, send, recv, seq, head):
    return pltpu.make_async_remote_copy(
        src_ref=src, dst_ref=dst, send_sem=send, recv_sem=recv,
        device_id=(seq, head), device_id_type=MESH,
    )


def greet(n, i, g, siblings):
    barrier = pltpu.get_barrier_semaphore()

    def say(p, c):
        pl.semaphore_signal(barrier, inc=1, device_id=(lax.rem(i + p, n), g), device_id_type=MESH)
        return c

    lax.fori_loop(1, n, say, 0)
    for h in siblings:
        pl.semaphore_signal(barrier, inc=1, device_id=(i, h), device_id_type=MESH)


def greeted(n):
    pl.semaphore_wait(pltpu.get_barrier_semaphore(), n + 2)


def rows_of(*parts):
    rows = list(parts)
    rows += [jnp.zeros_like(rows[0])] * (8 - len(rows))
    return jnp.concatenate(rows, axis=0)


def column_of(row):
    return jnp.transpose(jnp.broadcast_to(row, (LANES, LANES)))


def down(x):
    return jnp.sum(x, axis=0, keepdims=True)


def tables(n, nb, cap, i, ids, key_col, place_col, pos_row, target_row, tab):
    blocks, slots = n * nb, n * cap
    tiles = blocks // LANES
    per = LANES // nb
    lane = lax.broadcasted_iota(jnp.int32, (1, LANES), 1)
    across = lax.broadcasted_iota(jnp.int32, (LANES, LANES), 1)
    along = lax.broadcasted_iota(jnp.int32, (LANES, LANES), 0)
    earlier = along < across
    zero = jnp.zeros((1, LANES), jnp.int32)

    def keys(q, carry):
        total = ids[q * per]
        for o in range(1, per):
            total = total + ids[q * per + o]
        key = total * blocks + (q * LANES + lane)
        pos_row[q] = key
        for h in range(HG):
            key_col[q, h] = column_of(key[h:h + 1])
        return carry

    lax.fori_loop(0, tiles, keys, 0)

    def ranks(q, carry):
        key = pos_row[q]
        ranked = []
        for h in range(HG):
            def below(t, acc):
                return acc + down((key_col[t, h] < key[h:h + 1]).astype(jnp.int32))
            ranked.append(lax.fori_loop(0, tiles, below, zero))
        pos_row[q] = rows_of(*ranked)
        return carry

    lax.fori_loop(0, tiles, ranks, 0)

    def places(q, carry):
        inverse, code_at = carry
        pos = pos_row[q]
        owner = pos // nb
        src = (q * LANES + lane) // nb
        src_col = (q * LANES + along) // nb
        pair = owner + n * src
        pos_cols = [column_of(pos[h:h + 1]) for h in range(HG)]
        pair_cols = [p // nb + n * src_col for p in pos_cols]
        ks = []
        for h in range(HG):
            mine = pair[h:h + 1]
            k = down(((pair_cols[h] == mine) & earlier).astype(jnp.int32))
            for o in range(h):
                k = k + down((pair_cols[o] == mine).astype(jnp.int32))
            ks.append(k)
            k_col = column_of(k)
            place = jnp.where(pos_cols[h] // nb == i, src_col * cap + k_col, -1)
            code = pos_cols[h] + h * blocks
            place_col[q, h] = place
            key_col[q, h] = code
            code_at = code_at + down(jnp.where(place == across, code, 0))
            target = jnp.where(src_col == i, (pos_cols[h] // nb) * cap + k_col, -1)
            item = (along % nb) * HG + h
            inverse = inverse + down(jnp.where(target == across, item, 0))
        target_row[q] = jnp.minimum(owner * cap + rows_of(*ks), slots - 1)
        return inverse, code_at

    inverse, code_at = lax.fori_loop(0, tiles, places, (zero, zero))
    last_at = lane * blocks + i * nb + nb - 1

    def links(q, carry):
        before, tails = carry
        for h in range(HG):
            place, code = place_col[q, h], key_col[q, h]
            before = before + down(jnp.where((code == code_at - 1) & (place >= 0), place, 0))
            tails = tails + down(jnp.where((code == last_at) & (place >= 0), place, 0))
        return before, tails

    before, tails = lax.fori_loop(0, tiles, links, (zero, zero))
    before = jnp.where(code_at % nb == 0, slots + code_at // blocks, before)
    tab[...] = rows_of(jnp.minimum(inverse, nb * HG - 1), jnp.clip(before, 0, slots + HG - 1),
                       jnp.minimum(tails, slots - 1), jnp.clip(code_at // blocks, 0, HG - 1))


def main_kernel(n, cap, nb, buck_hbm, tok, ws_hbm, wv_hbm, wo_hbm, out,
                buck, sent, ids, key_col, place_col, pos_row, target_row, tab, idx, targets, goals,
                own, ws, wv, wo, wo_part, spread_v, g1, g2, g3, items_s, values, items_v, s_out, v_out,
                s_in, v_in0, v_in1, ts_out, ts_in, tv_out, tv_in, qbuf, kbuf, vbuf0, wbuf,
                out2, ans0, ans1, acc,
                local, wload, sg, rg, sx, rx, sc, rc, so, ro, ss, rs, sv, rv, st, rt,
                sr, rr, s1, r1, s2, r2, s3, r3):
    ans, v_in, vbuf = (ans0, ans1), (v_in0, v_in1), (vbuf0, qbuf)
    i = lax.axis_index("seq")
    g, h1, h2, h3 = head_ring()
    width = tok.shape[-1]
    slots = n * cap

    def part_of(c):
        return tok.at[:, pl.ds(c * ROWS, ROWS), :]

    loads = [pltpu.make_async_copy(src, dst, wload.at[k])
             for k, (src, dst) in enumerate(((ws_hbm, ws), (wv_hbm, wv), (wo_hbm, wo)))]
    own_loads = [pltpu.make_async_copy(part_of(c), own.at[c], local.at[c]) for c in range(PARTS)]
    greet(n, i, g, (h1, h2, h3))
    fetch = pltpu.make_async_copy(buck_hbm, buck, wload.at[3])
    fetch.start()
    loads[0].start()
    for load in own_loads:
        load.start()
    loads[1].start()
    loads[2].start()
    per = LANES // nb
    sent[...] = jnp.zeros_like(sent)
    fetch.wait()
    sent[:HG, :nb] = buck[...]
    sent[...] = pltpu.roll(sent[...], lax.rem(i, per) * nb, 1)
    ids[i] = sent[...]
    greeted(n)

    def bucket_copy(p):
        peer = lax.rem(i + p, n)
        return remote(sent, ids.at[i], sr.at[0, peer], rr.at[0, i], peer, g)

    def bucket_start(p, carry):
        bucket_copy(p).start()
        return carry

    lax.fori_loop(1, n, bucket_start, 0)

    def over_x(c):
        return remote(part_of(c), g2.at[c], sx.at[c], rx.at[c], i, h2)

    def over_core(c):
        return remote(part_of(c), g1.at[c], sc.at[c], rc.at[c], i, h1)

    def onward(c):
        return remote(g2.at[c], g3.at[c], so.at[c], ro.at[c], i, h1)

    for c in range(PARTS):
        over_x(c).start()
        over_core(c).start()

    def bucket_wait(p, carry):
        src = lax.rem(i + n - p, n)
        remote(sent, ids.at[src], sr.at[0, src], rr.at[0, src], src, g).wait()
        return carry

    lax.fori_loop(1, n, bucket_wait, 0)
    tables(n, nb, cap, i, ids, key_col, place_col, pos_row, target_row, tab)
    to_scalar = pltpu.make_async_copy(tab, idx, wload.at[3])
    to_scalar.start()
    targets[0] = target_row[lax.div(i, per)]
    goal_copies = [remote(targets.at[0], targets.at[r], sg.at[r], rg.at[r], i, h)
                   for r, h in ((1, h1), (2, h2), (3, h3))]
    for copy in goal_copies:
        copy.start()
    for load in loads:
        load.wait()
    for load in own_loads:
        load.wait()
    to_scalar.wait()

    def chunk(o):
        return pl.ds(o * cap, cap)

    def send_s(c, p):
        peer = lax.rem(i + p, n)
        return remote(s_out.at[c, peer], s_in.at[c, chunk(i)], ss.at[c], rs.at[c, i], peer, g)

    def send_v(q, p):
        peer = lax.rem(i + p, n)
        return remote(v_out.at[q, peer], v_in[q].at[chunk(i)], sv.at[q], rv.at[q, i], peer, g)

    low = lax.broadcasted_iota(jnp.int32, (FOLD, 2 * DH), 1) < DH
    group_at = lax.broadcasted_iota(jnp.int32, (QROWS, QUART * DV), 1) // DV
    query_scale = jnp.where(lax.broadcasted_iota(jnp.int32, (1, 2 * DH), 1) < DH,
                            jnp.float32(DH ** -0.5), jnp.float32(0.0))

    def unfold(x):
        x = x.astype(jnp.float32)
        turned = pltpu.roll(x, DH, 1)
        return jnp.concatenate([jnp.where(low, x, turned), jnp.where(low, turned, x)], axis=0)

    def khat_of(x):
        square = jnp.sum(x * x, axis=1, keepdims=True) * (0.5 / DH)
        return (x * lax.rsqrt(square + 1e-6)).astype(jnp.bfloat16)

    step_blocks = min(nb, 8)

    def project(c, w, store):
        def one(q, carry):
            total = jnp.zeros((step_blocks * ROWS, HG * DH), jnp.float32)
            for ref, h in ((own, g), (g1, h1), (g2, h2), (g3, h3)):
                x = ref[c, pl.ds(q * step_blocks, step_blocks)].reshape(step_blocks * ROWS, width)
                total += jnp.dot(x, w[pl.ds(pl.multiple_of(h * width, width), width), :],
                                 preferred_element_type=jnp.float32)
            store(c, q * step_blocks, total.astype(jnp.bfloat16))
            return carry

        lax.fori_loop(0, nb // step_blocks, one, 0)

    def store_s(c, at, full):
        for b in range(step_blocks):
            for h in range(HG):
                cols = slice(h * DH, (h + 1) * DH)
                items_s[c, (at + b) * HG + h] = jnp.concatenate(
                    [full[b * ROWS: b * ROWS + FOLD, cols],
                     full[b * ROWS + FOLD: (b + 1) * ROWS, cols]], axis=1)

    def store_v(c, at, full):
        values[pl.ds(at, step_blocks), pl.ds(pl.multiple_of(c * ROWS, ROWS), ROWS)] = (
            full.reshape(step_blocks, ROWS, HG * DH))

    def ready_s(c, o):
        rows = pl.ds(pl.multiple_of(c * ROWS, ROWS), ROWS)
        for k in range(cap):
            j = o * cap + k
            x = unfold(s_in[c, j])
            qbuf[j, rows] = (x * query_scale).astype(jnp.bfloat16)
            kbuf[j, rows] = khat_of(x)

    def arrive_s(c):
        ready_s(c, i)

        def one(p, carry):
            src = lax.rem(i + n - p, n)
            remote(s_out.at[c, src], s_in.at[c, chunk(src)], ss.at[c], rs.at[c, src], src, g).wait_recv()
            ready_s(c, src)
            return carry

        lax.fori_loop(1, n, one, 0)

    def gather(c, carry):
        over_x(c).wait_recv()
        onward(c).start()
        over_core(c).wait_recv()
        onward(c).wait_recv()
        project(c, ws, store_s)

        def pack(p, carry):
            peer = lax.rem(i + p, n)
            for k in range(cap):
                s_out[c, peer, k] = items_s[c, idx[0, peer * cap + k]]
            send_s(c, p).start()
            return carry

        lax.fori_loop(1, n, pack, 0)
        for k in range(cap):
            s_in[c, i * cap + k] = items_s[c, idx[0, i * cap + k]]
        project(c, wv, store_v)

        @pl.when(c > 0)
        def _():
            arrive_s(c - 1)
        return carry

    lax.fori_loop(0, PARTS, gather, 0)

    def build_v(q):
        def one(b, carry):
            for h in range(HG):
                cols = slice(h * DH + q * DV, h * DH + (q + 1) * DV)
                items_v[q, b * HG + h] = jnp.concatenate(
                    [values[b, t * QROWS:(t + 1) * QROWS, cols] for t in range(QUART)], axis=1)
            return carry

        lax.fori_loop(0, nb, one, 0)

        def pack(p, carry):
            peer = lax.rem(i + p, n)
            for k in range(cap):
                v_out[q, peer, k] = items_v[q, idx[0, peer * cap + k]]
            return carry

        lax.fori_loop(1, n, pack, 0)
        for k in range(cap):
            v_in[q][i * cap + k] = items_v[q, idx[0, i * cap + k]]

    build_v(0)

    def start_v(p, carry):
        send_v(0, p).start()
        return carry

    lax.fori_loop(1, n, start_v, 0)
    arrive_s(PARTS - 1)

    for h in range(HG):
        at = idx[2, h]
        for c in range(PARTS):
            ts_out[h, c] = s_in[c, at]
    following = lax.rem(i + 1, n)
    tail_s = remote(ts_out, ts_in, st.at[0], rt.at[0], following, g)
    tail_s.start()

    build_v(1)
    l_at = lax.broadcasted_iota(jnp.int32, (QUART * DV, QUART * QUART * DV), 0)
    w_at = lax.broadcasted_iota(jnp.int32, (QUART * DV, QUART * QUART * DV), 1)
    spread_v[...] = ((l_at // DV == w_at // (QUART * DV)) & (l_at % DV == w_at % DV)).astype(
        jnp.float32).astype(jnp.bfloat16)

    def ready_v(q, x, at, count):
        wide = jnp.dot(x.reshape(count * QROWS, QUART * DV), spread_v[...],
                       preferred_element_type=jnp.float32).astype(jnp.bfloat16)
        for t in range(QUART):
            vbuf[q][pl.ds(at, count), t * QROWS:(t + 1) * QROWS] = (
                wide[:, t * QUART * DV:(t + 1) * QUART * DV].reshape(count, QROWS, QUART * DV))

    def ready_v_of(q, o):
        ready_v(q, v_in[q][chunk(o)], o * cap, cap)

    ready_v_of(0, i)
    for r, h in enumerate((g, h1, h2, h3)):
        for q in range(HALVES):
            for t in range(QUART):
                for c in range(QUART):
                    src = pl.multiple_of(h * HG * DH, HG * DH) + (c ^ t) * DH + q * DV
                    wo_part[q, t, (r * QUART + c) * DV:(r * QUART + c + 1) * DV] = wo[pl.ds(src, DV), :]
    tail_s.wait_recv()
    for h in range(HG):
        for c in range(PARTS):
            kbuf[slots + h, c * ROWS:(c + 1) * ROWS] = khat_of(unfold(ts_in[h, c]))

    row_at = lax.broadcasted_iota(jnp.int32, (BLK, 2 * BLK), 0)
    col_at = lax.broadcasted_iota(jnp.int32, (BLK, 2 * BLK), 1)
    itself = col_at == row_at + BLK

    def weigh(o, carry):
        for k in range(cap):
            j = o * cap + k
            keys = jnp.concatenate([kbuf[idx[1, j]], kbuf[j]], axis=0)
            scores = lax.dot_general(qbuf[j], keys, (((1,), (1,)), ((), ())),
                                     preferred_element_type=jnp.float32)
            scores = jnp.where(itself, jnp.float32(-100000.0), scores)
            expo = jnp.exp(scores - jnp.max(scores, axis=1, keepdims=True))
            wbuf[j] = (expo * (1.0 / jnp.sum(expo, axis=1, keepdims=True))).astype(jnp.bfloat16)
        return carry

    lax.fori_loop(0, n, weigh, 0)
    for copy in goal_copies:
        copy.wait_recv()
    goal_scalar = pltpu.make_async_copy(targets, goals, wload.at[3])
    goal_scalar.start()

    def take_v(q, src):
        remote(v_out.at[q, src], v_in[q].at[chunk(src)], sv.at[q], rv.at[q, src], src, g).wait_recv()

    def pass_tail(q):
        for h in range(HG):
            tv_out[q, h] = v_in[q][idx[2, h]]
        tail_v(q).start()

    def take_tail(q):
        tail_v(q).wait_recv()
        ready_v(q, tv_in[q], slots, HG)

    def tail_v(q):
        return remote(tv_out.at[q], tv_in.at[q], st.at[1 + q], rt.at[1 + q], following, g)

    def attend(q, j):
        keyed = jnp.concatenate([vbuf[q][idx[1, j]], vbuf[q][j]], axis=0)
        mixed = jnp.dot(wbuf[j], keyed, preferred_element_type=jnp.float32)
        turn = group_at ^ idx[3, j]
        picked = mixed[(QUART - 1) * QROWS:]
        for t in range(QUART - 1):
            picked = jnp.where(turn == t, mixed[t * QROWS:(t + 1) * QROWS], picked)
        return picked.astype(jnp.bfloat16)

    def answers_of(e, r, o):
        return ans[e].at[r, chunk(o)]

    def reply(e, p):
        peer = lax.rem(i + p, n)
        return remote(out2.at[e, peer], answers_of(e, 0, i), sr.at[e, 0], rr.at[e, i], peer, g)

    def whole(e, r):
        return ans[e].at[r]

    def relay1(e):
        return remote(whole(e, 0), whole(e, 1), s1.at[e], r1.at[e], i, h1)

    def relay2(e, o):
        return remote(answers_of(e, 0, o), answers_of(e, 2, o), s2.at[e], r2.at[e], i, h2)

    def relay2_all(e):
        return remote(whole(e, 0), whole(e, 2), s2.at[e], r2.at[e], i, h2)

    def relay3(e):
        return remote(whole(e, 2), whole(e, 3), s3.at[e], r3.at[e], i, h1)

    def source(p):
        return lax.rem(i + n - p, n)

    def answer(q, p):
        peer = lax.rem(i + p, n)
        for k in range(cap):
            out2[q, peer, k] = attend(q, peer * cap + k)
        reply(q, p).start()

    def relay(e, p):
        src = source(p)
        remote(out2.at[e, src], answers_of(e, 0, src), sr.at[e, 0], rr.at[e, src], src, g).wait_recv()
        relay2(e, src).start()

    def spread(e):
        relay2_all(e).wait_recv()
        relay3(e).start()

    def own_answer(q):
        for k in range(cap):
            ans[q][0, i * cap + k] = attend(q, i * cap + k)
        relay2(q, i).start()

    def settle(e):
        relay1(e).wait_recv()
        relay3(e).wait_recv()

    def relays_sent(e):
        relay1(e).wait_send()
        relay2_all(e).wait_send()
        relay3(e).wait_send()

    following_peer = lax.rem(i + 1, n)

    def replies_sent(e):
        block = out2.at[e, pl.ds(0, n - 1)]
        remote(block, block, sr.at[e, 0], rr.at[e, 0], following_peer, g).wait_send()

    def values_sent(q):
        block = v_out.at[q, pl.ds(0, n - 1)]
        remote(block, block, sv.at[q], rv.at[q, 0], following_peer, g).wait_send()

    def shared_sent(c):
        block = s_out.at[c, pl.ds(0, n - 1)]
        remote(block, block, ss.at[c], rs.at[c, 0], following_peer, g).wait_send()

    goal_scalar.wait()
    mixing = (g1, g3)

    def finish(q):
        def assemble(b, carry):
            for r in range(HG):
                parts = [ans[q][r, goals[r, k, lax.rem(i, per) * nb + b]] for k in range(HG)]
                cols = slice((r % 2) * QUART * DV, (r % 2 + 1) * QUART * DV)
                for t in range(QUART):
                    tile = parts[(QUART - 1) ^ t]
                    for c in range(QUART - 1):
                        tile = jnp.where(group_at == c, parts[c ^ t], tile)
                    mixing[r // 2][t, b, :, cols] = tile
            return carry

        lax.fori_loop(0, nb, assemble, 0)
        depth = 2 * QUART * DV
        for t in range(QUART):
            total = jnp.zeros((nb * QROWS, width), jnp.float32)
            for c in range(HG // 2):
                total += jnp.dot(mixing[c][t].reshape(nb * QROWS, depth), wo_part[q, t, c * depth:(c + 1) * depth],
                                 preferred_element_type=jnp.float32)
            if q == 0:
                acc[t] = own[t].reshape(nb * QROWS, width).astype(jnp.float32) + total
            else:
                out[:, t * QROWS:(t + 1) * QROWS] = (acc[t] + total).astype(jnp.bfloat16).reshape(nb, QROWS, width)

    def each(body, first=1, last=n):
        def one(p, carry):
            odd = lax.rem(p, 2)
            body(odd * lax.div(p + 1, 2) + (1 - odd) * (n - lax.div(p, 2)))
            return carry

        lax.fori_loop(first, last, one, 0)

    def first_values(p):
        take_v(0, source(p))
        send_v(1, p).start()
        ready_v_of(0, source(p))

    def second_values(p):
        take_v(1, source(p))
        ready_v_of(1, source(p))

    for c in range(PARTS):
        over_x(c).wait_send()
        over_core(c).wait_send()
        onward(c).wait_send()
        shared_sent(c)
    for copy in goal_copies:
        copy.wait_send()
    each(first_values)
    pass_tail(0)
    ready_v_of(1, i)
    tail_s.wait_send()
    take_tail(0)
    own_answer(0)
    each(lambda p: answer(0, p))
    values_sent(0)
    mid = n // 2 + 1
    each(second_values)
    pass_tail(1)
    each(lambda p: relay(0, p), 1, mid)
    take_tail(1)
    own_answer(1)
    each(lambda p: answer(1, p))
    each(lambda p: relay(0, p), mid)
    relay1(0).start()
    values_sent(1)

    def turn_over(p):
        relay(1, p)

    each(turn_over, 1, mid)
    spread(0)
    each(turn_over, mid)
    relay1(1).start()
    replies_sent(0)
    settle(0)
    finish(0)
    relays_sent(0)
    spread(1)
    replies_sent(1)
    for q in range(HALVES):
        tail_v(q).wait_send()
    settle(1)
    finish(1)
    relays_sent(1)


def per_device(tokens, buckets, w_shared, w_value, w_output):
    n = lax.axis_size("seq")
    nb = buckets.shape[0]
    rows, width = tokens.shape
    cap = max(1, nb * HG // n)
    slots = n * cap
    bf = jnp.bfloat16
    vmem = pl.BlockSpec(memory_space=pltpu.VMEM)
    tiles = n * nb // LANES
    i32 = jnp.int32
    square = pltpu.VMEM((tiles, HG, LANES, LANES), i32)
    line = pltpu.VMEM((tiles, 8, LANES), i32)
    hbm = pl.BlockSpec(memory_space=pltpu.HBM)
    dma = lambda *k: pltpu.SemaphoreType.DMA(k)
    gathered = pltpu.VMEM((PARTS, nb, ROWS, width), bf)
    weight = pltpu.VMEM(w_shared.shape, bf)
    small = (FOLD, 2 * DH)
    quarter = (QROWS, QUART * DV)
    out = pl.pallas_call(
        functools.partial(main_kernel, n, cap, nb),
        out_shape=jax.ShapeDtypeStruct((nb, BLK, width), bf),
        in_specs=[hbm] * 5,
        out_specs=vmem,
        scratch_shapes=[pltpu.VMEM((HG, nb), i32), pltpu.VMEM((8, LANES), i32), pltpu.VMEM((n, 8, LANES), i32)]
        + [square] * 2 + [line] * 2
        + [pltpu.VMEM((8, LANES), i32), pltpu.SMEM((8, LANES), i32)]
        + [pltpu.VMEM((HG, 8, LANES), i32), pltpu.SMEM((HG, 8, LANES), i32)]
        + [gathered] + [weight] * 3
        + [pltpu.VMEM((HALVES, QUART, HG * QUART * DV, width), bf), pltpu.VMEM((QUART * DV, QUART * QUART * DV), bf)]
        + [gathered] * 3
        + [pltpu.VMEM((PARTS, nb * HG) + small, bf), pltpu.VMEM((nb, BLK, HG * DH), bf)]
        + [pltpu.VMEM((HALVES, nb * HG) + quarter, bf)]
        + [pltpu.VMEM((PARTS, n, cap) + small, bf), pltpu.VMEM((HALVES, n, cap) + quarter, bf)]
        + [pltpu.VMEM((PARTS, slots) + small, bf)] + [pltpu.VMEM((slots,) + quarter, bf)] * 2
        + [pltpu.VMEM((HG, PARTS) + small, bf)] * 2
        + [pltpu.VMEM((HALVES, HG) + quarter, bf)] * 2
        + [pltpu.VMEM((slots + HG, BLK, 2 * DH), bf)] * 3
        + [pltpu.VMEM((slots, BLK, 2 * BLK), bf)]
        + [pltpu.VMEM((HALVES, n, cap) + quarter, bf)] + [pltpu.VMEM((HG, slots) + quarter, bf)] * 2
        + [pltpu.VMEM((QUART, nb * QROWS, width), jnp.float32)]
        + [dma(PARTS), dma(4)] + [dma(HG)] * 2 + [dma(PARTS)] * 6 + [dma(PARTS), dma(PARTS, n), dma(HALVES), dma(HALVES, n)] + [dma(1 + HALVES)] * 2
        + [dma(HALVES, n)] * 2 + [dma(HALVES)] * 6,
        compiler_params=pltpu.CompilerParams(collective_id=0, has_side_effects=True,
                                             vmem_limit_bytes=62 << 20),
    )(buckets.T, tokens.reshape(nb, BLK, width), w_shared, w_value, w_output)
    return out.reshape(rows, width)


def solution(mesh):
    return jax.shard_map(
        per_device,
        mesh=mesh,
        in_specs=(
            P("seq", "head"),
            P("seq", "head"),
            P(None, "head"),
            P(None, "head"),
            P(None, "head"),
        ),
        out_specs=P("seq", "head"),
        check_vma=False,
    )
```

```python
import functools

import jax
import jax.numpy as jnp
from jax import lax
from jax.experimental import pallas as pl
from jax.experimental.pallas import tpu as pltpu
from jax.sharding import PartitionSpec as P

DH = 64
BLK = 128
HG = 4
LANES = 128
PARTS = 4
ROWS = BLK // PARTS
FOLD = ROWS // 2
HALVES = 2
DV = DH // HALVES
QUART = 4
QROWS = BLK // QUART
MESH = pl.DeviceIdType.MESH


def head_ring():
    g = lax.axis_index("head")
    h1 = g + 1 - 2 * lax.rem(g, 2)
    h2 = g + 2 - 4 * lax.div(g, 2)
    h3 = h1 + 2 - 4 * lax.div(h1, 2)
    return g, h1, h2, h3


def remote(src, dst, send, recv, seq, head):
    return pltpu.make_async_remote_copy(
        src_ref=src, dst_ref=dst, send_sem=send, recv_sem=recv,
        device_id=(seq, head), device_id_type=MESH,
    )


def greet(n, i, g, siblings):
    barrier = pltpu.get_barrier_semaphore()

    def say(p, c):
        pl.semaphore_signal(barrier, inc=1, device_id=(lax.rem(i + p, n), g), device_id_type=MESH)
        return c

    lax.fori_loop(1, n, say, 0)
    for h in siblings:
        pl.semaphore_signal(barrier, inc=1, device_id=(i, h), device_id_type=MESH)


def greeted(n):
    pl.semaphore_wait(pltpu.get_barrier_semaphore(), n + 2)


def rows_of(*parts):
    rows = list(parts)
    rows += [jnp.zeros_like(rows[0])] * (8 - len(rows))
    return jnp.concatenate(rows, axis=0)


def column_of(row):
    return jnp.transpose(jnp.broadcast_to(row, (LANES, LANES)))


def down(x):
    return jnp.sum(x, axis=0, keepdims=True)


def tables(n, nb, cap, i, ids, key_col, place_col, pos_row, target_row, tab):
    blocks, slots = n * nb, n * cap
    tiles = blocks // LANES
    per = LANES // nb
    lane = lax.broadcasted_iota(jnp.int32, (1, LANES), 1)
    across = lax.broadcasted_iota(jnp.int32, (LANES, LANES), 1)
    along = lax.broadcasted_iota(jnp.int32, (LANES, LANES), 0)
    earlier = along < across
    zero = jnp.zeros((1, LANES), jnp.int32)

    def keys(q, carry):
        total = ids[q * per]
        for o in range(1, per):
            total = total + ids[q * per + o]
        key = total * blocks + (q * LANES + lane)
        pos_row[q] = key
        for h in range(HG):
            key_col[q, h] = column_of(key[h:h + 1])
        return carry

    lax.fori_loop(0, tiles, keys, 0)

    def ranks(q, carry):
        key = pos_row[q]
        ranked = []
        for h in range(HG):
            def below(t, acc):
                return acc + down((key_col[t, h] < key[h:h + 1]).astype(jnp.int32))
            ranked.append(lax.fori_loop(0, tiles, below, zero))
        pos_row[q] = rows_of(*ranked)
        return carry

    lax.fori_loop(0, tiles, ranks, 0)

    def places(q, carry):
        inverse, code_at = carry
        pos = pos_row[q]
        owner = pos // nb
        src = (q * LANES + lane) // nb
        src_col = (q * LANES + along) // nb
        pair = owner + n * src
        pos_cols = [column_of(pos[h:h + 1]) for h in range(HG)]
        pair_cols = [p // nb + n * src_col for p in pos_cols]
        ks = []
        for h in range(HG):
            mine = pair[h:h + 1]
            k = down(((pair_cols[h] == mine) & earlier).astype(jnp.int32))
            for o in range(h):
                k = k + down((pair_cols[o] == mine).astype(jnp.int32))
            ks.append(k)
            k_col = column_of(k)
            place = jnp.where(pos_cols[h] // nb == i, src_col * cap + k_col, -1)
            code = pos_cols[h] + h * blocks
            place_col[q, h] = place
            key_col[q, h] = code
            code_at = code_at + down(jnp.where(place == across, code, 0))
            target = jnp.where(src_col == i, (pos_cols[h] // nb) * cap + k_col, -1)
            item = (along % nb) * HG + h
            inverse = inverse + down(jnp.where(target == across, item, 0))
        target_row[q] = jnp.minimum(owner * cap + rows_of(*ks), slots - 1)
        return inverse, code_at

    inverse, code_at = lax.fori_loop(0, tiles, places, (zero, zero))
    last_at = lane * blocks + i * nb + nb - 1

    def links(q, carry):
        before, tails = carry
        for h in range(HG):
            place, code = place_col[q, h], key_col[q, h]
            before = before + down(jnp.where((code == code_at - 1) & (place >= 0), place, 0))
            tails = tails + down(jnp.where((code == last_at) & (place >= 0), place, 0))
        return before, tails

    before, tails = lax.fori_loop(0, tiles, links, (zero, zero))
    before = jnp.where(code_at % nb == 0, slots + code_at // blocks, before)
    tab[...] = rows_of(jnp.minimum(inverse, nb * HG - 1), jnp.clip(before, 0, slots + HG - 1),
                       jnp.minimum(tails, slots - 1), jnp.clip(code_at // blocks, 0, HG - 1))


def main_kernel(n, cap, nb, buck_hbm, tok, ws_hbm, wv_hbm, wo_hbm, out,
                buck, sent, ids, key_col, place_col, pos_row, target_row, tab, idx, targets, goals,
                own, ws, wv, wo, wo_part, spread_v, g1, g2, g3, items_s, values, items_v, s_out, v_out,
                s_in, v_in0, v_in1, ts_out, ts_in, tv_out, tv_in, qbuf, kbuf, vbuf0, wbuf,
                out2, a00, a01, a02, a03, a10, a11, a12, a13, acc,
                local, wload, sg, rg, sx, rx, sc, rc, so, ro, ss, rs, sv, rv, st, rt,
                sr, rr, s1, r1, s2, r2, s3, r3):
    ans, v_in, vbuf = ((a00, a01, a02, a03), (a10, a11, a12, a13)), (v_in0, v_in1), (vbuf0, qbuf)
    i = lax.axis_index("seq")
    g, h1, h2, h3 = head_ring()
    width = tok.shape[-1]
    slots = n * cap

    def part_of(c):
        return tok.at[:, pl.ds(c * ROWS, ROWS), :]

    loads = [pltpu.make_async_copy(src, dst, wload.at[k])
             for k, (src, dst) in enumerate(((ws_hbm, ws), (wv_hbm, wv), (wo_hbm, wo)))]
    own_loads = [pltpu.make_async_copy(part_of(c), own.at[c], local.at[c]) for c in range(PARTS)]
    greet(n, i, g, (h1, h2, h3))
    fetch = pltpu.make_async_copy(buck_hbm, buck, wload.at[3])
    fetch.start()
    loads[0].start()
    for load in own_loads:
        load.start()
    loads[1].start()
    loads[2].start()
    per = LANES // nb
    sent[...] = jnp.zeros_like(sent)
    fetch.wait()
    sent[:HG, :nb] = buck[...]
    sent[...] = pltpu.roll(sent[...], lax.rem(i, per) * nb, 1)
    ids[i] = sent[...]
    greeted(n)

    def bucket_copy(p):
        peer = lax.rem(i + p, n)
        return remote(sent, ids.at[i], sr.at[0, peer], rr.at[0, i], peer, g)

    def bucket_start(p, carry):
        bucket_copy(p).start()
        return carry

    lax.fori_loop(1, n, bucket_start, 0)

    def over_x(c):
        return remote(part_of(c), g2.at[c], sx.at[c], rx.at[c], i, h2)

    def over_core(c):
        return remote(part_of(c), g1.at[c], sc.at[c], rc.at[c], i, h1)

    def onward(c):
        return remote(g2.at[c], g3.at[c], so.at[c], ro.at[c], i, h1)

    for c in range(PARTS):
        over_x(c).start()
        over_core(c).start()

    def bucket_wait(p, carry):
        src = lax.rem(i + n - p, n)
        remote(sent, ids.at[src], sr.at[0, src], rr.at[0, src], src, g).wait()
        return carry

    lax.fori_loop(1, n, bucket_wait, 0)
    tables(n, nb, cap, i, ids, key_col, place_col, pos_row, target_row, tab)
    to_scalar = pltpu.make_async_copy(tab, idx, wload.at[3])
    to_scalar.start()
    targets[0] = target_row[lax.div(i, per)]
    goal_copies = [remote(targets.at[0], targets.at[r], sg.at[r], rg.at[r], i, h)
                   for r, h in ((1, h1), (2, h2), (3, h3))]
    for copy in goal_copies:
        copy.start()
    for load in loads:
        load.wait()
    for load in own_loads:
        load.wait()
    to_scalar.wait()

    def chunk(o):
        return pl.ds(o * cap, cap)

    def send_s(c, p):
        peer = lax.rem(i + p, n)
        return remote(s_out.at[c, peer], s_in.at[c, chunk(i)], ss.at[c], rs.at[c, i], peer, g)

    def send_v(q, p):
        peer = lax.rem(i + p, n)
        return remote(v_out.at[q, peer], v_in[q].at[chunk(i)], sv.at[q], rv.at[q, i], peer, g)

    low = lax.broadcasted_iota(jnp.int32, (FOLD, 2 * DH), 1) < DH
    group_at = lax.broadcasted_iota(jnp.int32, (QROWS, QUART * DV), 1) // DV
    query_scale = jnp.where(lax.broadcasted_iota(jnp.int32, (1, 2 * DH), 1) < DH,
                            jnp.float32(DH ** -0.5), jnp.float32(0.0))

    def unfold(x):
        x = x.astype(jnp.float32)
        turned = pltpu.roll(x, DH, 1)
        return jnp.concatenate([jnp.where(low, x, turned), jnp.where(low, turned, x)], axis=0)

    def khat_of(x):
        square = jnp.sum(x * x, axis=1, keepdims=True) * (0.5 / DH)
        return (x * lax.rsqrt(square + 1e-6)).astype(jnp.bfloat16)

    step_blocks = min(nb, 8)

    def project(c, w, store):
        def one(q, carry):
            total = jnp.zeros((step_blocks * ROWS, HG * DH), jnp.float32)
            for ref, h in ((own, g), (g1, h1), (g2, h2), (g3, h3)):
                x = ref[c, pl.ds(q * step_blocks, step_blocks)].reshape(step_blocks * ROWS, width)
                total += jnp.dot(x, w[pl.ds(pl.multiple_of(h * width, width), width), :],
                                 preferred_element_type=jnp.float32)
            store(c, q * step_blocks, total.astype(jnp.bfloat16))
            return carry

        lax.fori_loop(0, nb // step_blocks, one, 0)

    def store_s(c, at, full):
        for b in range(step_blocks):
            for h in range(HG):
                cols = slice(h * DH, (h + 1) * DH)
                items_s[c, (at + b) * HG + h] = jnp.concatenate(
                    [full[b * ROWS: b * ROWS + FOLD, cols],
                     full[b * ROWS + FOLD: (b + 1) * ROWS, cols]], axis=1)

    def store_v(c, at, full):
        values[pl.ds(at, step_blocks), pl.ds(pl.multiple_of(c * ROWS, ROWS), ROWS)] = (
            full.reshape(step_blocks, ROWS, HG * DH))

    def ready_s(c, o):
        rows = pl.ds(pl.multiple_of(c * ROWS, ROWS), ROWS)
        for k in range(cap):
            j = o * cap + k
            x = unfold(s_in[c, j])
            qbuf[j, rows] = (x * query_scale).astype(jnp.bfloat16)
            kbuf[j, rows] = khat_of(x)

    def arrive_s(c):
        ready_s(c, i)

        def one(p, carry):
            src = lax.rem(i + n - p, n)
            remote(s_out.at[c, src], s_in.at[c, chunk(src)], ss.at[c], rs.at[c, src], src, g).wait_recv()
            ready_s(c, src)
            return carry

        lax.fori_loop(1, n, one, 0)

    def gather(c, carry):
        over_x(c).wait_recv()
        onward(c).start()
        over_core(c).wait_recv()
        onward(c).wait_recv()
        project(c, ws, store_s)

        def pack(p, carry):
            peer = lax.rem(i + p, n)
            for k in range(cap):
                s_out[c, peer, k] = items_s[c, idx[0, peer * cap + k]]
            send_s(c, p).start()
            return carry

        lax.fori_loop(1, n, pack, 0)
        for k in range(cap):
            s_in[c, i * cap + k] = items_s[c, idx[0, i * cap + k]]
        project(c, wv, store_v)

        @pl.when(c > 0)
        def _():
            arrive_s(c - 1)
        return carry

    lax.fori_loop(0, PARTS, gather, 0)

    def build_v(q):
        def one(b, carry):
            for h in range(HG):
                cols = slice(h * DH + q * DV, h * DH + (q + 1) * DV)
                items_v[q, b * HG + h] = jnp.concatenate(
                    [values[b, t * QROWS:(t + 1) * QROWS, cols] for t in range(QUART)], axis=1)
            return carry

        lax.fori_loop(0, nb, one, 0)

        def pack(p, carry):
            peer = lax.rem(i + p, n)
            for k in range(cap):
                v_out[q, peer, k] = items_v[q, idx[0, peer * cap + k]]
            return carry

        lax.fori_loop(1, n, pack, 0)
        for k in range(cap):
            v_in[q][i * cap + k] = items_v[q, idx[0, i * cap + k]]

    build_v(0)

    def start_v(p, carry):
        send_v(0, p).start()
        return carry

    lax.fori_loop(1, n, start_v, 0)
    arrive_s(PARTS - 1)

    for h in range(HG):
        at = idx[2, h]
        for c in range(PARTS):
            ts_out[h, c] = s_in[c, at]
    following = lax.rem(i + 1, n)
    tail_s = remote(ts_out, ts_in, st.at[0], rt.at[0], following, g)
    tail_s.start()

    build_v(1)
    l_at = lax.broadcasted_iota(jnp.int32, (QUART * DV, QUART * QUART * DV), 0)
    w_at = lax.broadcasted_iota(jnp.int32, (QUART * DV, QUART * QUART * DV), 1)
    spread_v[...] = ((l_at // DV == w_at // (QUART * DV)) & (l_at % DV == w_at % DV)).astype(
        jnp.float32).astype(jnp.bfloat16)

    def ready_v(q, x, at, count):
        wide = jnp.dot(x.reshape(count * QROWS, QUART * DV), spread_v[...],
                       preferred_element_type=jnp.float32).astype(jnp.bfloat16)
        for t in range(QUART):
            vbuf[q][pl.ds(at, count), t * QROWS:(t + 1) * QROWS] = (
                wide[:, t * QUART * DV:(t + 1) * QUART * DV].reshape(count, QROWS, QUART * DV))

    def ready_v_of(q, o):
        ready_v(q, v_in[q][chunk(o)], o * cap, cap)

    ready_v_of(0, i)
    for r, h in enumerate((g, h1, h2, h3)):
        for q in range(HALVES):
            for t in range(QUART):
                for c in range(QUART):
                    src = pl.multiple_of(h * HG * DH, HG * DH) + (c ^ t) * DH + q * DV
                    wo_part[q, t, (r * QUART + c) * DV:(r * QUART + c + 1) * DV] = wo[pl.ds(src, DV), :]
    tail_s.wait_recv()
    for h in range(HG):
        for c in range(PARTS):
            kbuf[slots + h, c * ROWS:(c + 1) * ROWS] = khat_of(unfold(ts_in[h, c]))

    row_at = lax.broadcasted_iota(jnp.int32, (BLK, 2 * BLK), 0)
    col_at = lax.broadcasted_iota(jnp.int32, (BLK, 2 * BLK), 1)
    itself = col_at == row_at + BLK

    def weigh(o, carry):
        for k in range(cap):
            j = o * cap + k
            keys = jnp.concatenate([kbuf[idx[1, j]], kbuf[j]], axis=0)
            scores = lax.dot_general(qbuf[j], keys, (((1,), (1,)), ((), ())),
                                     preferred_element_type=jnp.float32)
            scores = jnp.where(itself, jnp.float32(-100000.0), scores)
            expo = jnp.exp(scores - jnp.max(scores, axis=1, keepdims=True))
            wbuf[j] = (expo * (1.0 / jnp.sum(expo, axis=1, keepdims=True))).astype(jnp.bfloat16)
        return carry

    lax.fori_loop(0, n, weigh, 0)
    for copy in goal_copies:
        copy.wait_recv()
    goal_scalar = pltpu.make_async_copy(targets, goals, wload.at[3])
    goal_scalar.start()

    def take_v(q, src):
        remote(v_out.at[q, src], v_in[q].at[chunk(src)], sv.at[q], rv.at[q, src], src, g).wait_recv()

    def pass_tail(q):
        for h in range(HG):
            tv_out[q, h] = v_in[q][idx[2, h]]
        tail_v(q).start()

    def take_tail(q):
        tail_v(q).wait_recv()
        ready_v(q, tv_in[q], slots, HG)

    def tail_v(q):
        return remote(tv_out.at[q], tv_in.at[q], st.at[1 + q], rt.at[1 + q], following, g)

    def attend(q, j):
        keyed = jnp.concatenate([vbuf[q][idx[1, j]], vbuf[q][j]], axis=0)
        mixed = jnp.dot(wbuf[j], keyed, preferred_element_type=jnp.float32)
        turn = group_at ^ idx[3, j]
        picked = mixed[(QUART - 1) * QROWS:]
        for t in range(QUART - 1):
            picked = jnp.where(turn == t, mixed[t * QROWS:(t + 1) * QROWS], picked)
        return picked.astype(jnp.bfloat16)

    def answers_of(e, r, o):
        return ans[e][r].at[chunk(o)]

    def reply(e, p):
        peer = lax.rem(i + p, n)
        return remote(out2.at[e, peer], answers_of(e, 0, i), sr.at[e, 0], rr.at[e, i], peer, g)

    def whole(e, r):
        return ans[e][r]

    def relay1(e):
        return remote(whole(e, 0), whole(e, 1), s1.at[e], r1.at[e], i, h1)

    def relay2(e, o):
        return remote(answers_of(e, 0, o), answers_of(e, 2, o), s2.at[e], r2.at[e], i, h2)

    def relay2_all(e):
        return remote(whole(e, 0), whole(e, 2), s2.at[e], r2.at[e], i, h2)

    def relay3(e):
        return remote(whole(e, 2), whole(e, 3), s3.at[e], r3.at[e], i, h1)

    def source(p):
        return lax.rem(i + n - p, n)

    def answer(q, p):
        peer = lax.rem(i + p, n)
        for k in range(cap):
            out2[q, peer, k] = attend(q, peer * cap + k)
        reply(q, p).start()

    def relay(e, p):
        src = source(p)
        remote(out2.at[e, src], answers_of(e, 0, src), sr.at[e, 0], rr.at[e, src], src, g).wait_recv()
        relay2(e, src).start()

    def spread(e):
        relay2_all(e).wait_recv()
        relay3(e).start()

    def own_answer(q):
        for k in range(cap):
            ans[q][0][i * cap + k] = attend(q, i * cap + k)
        relay2(q, i).start()

    def relays_sent(e):
        relay1(e).wait_send()
        relay2_all(e).wait_send()
        relay3(e).wait_send()

    following_peer = lax.rem(i + 1, n)

    def replies_sent(e):
        block = out2.at[e, pl.ds(0, n - 1)]
        remote(block, block, sr.at[e, 0], rr.at[e, 0], following_peer, g).wait_send()

    def values_sent(q):
        block = v_out.at[q, pl.ds(0, n - 1)]
        remote(block, block, sv.at[q], rv.at[q, 0], following_peer, g).wait_send()

    def shared_sent(c):
        block = s_out.at[c, pl.ds(0, n - 1)]
        remote(block, block, ss.at[c], rs.at[c, 0], following_peer, g).wait_send()

    goal_scalar.wait()
    mixing = (g1, g3)

    depth = 2 * QUART * DV

    def assemble(q, ranks):
        def one(b, carry):
            for r in ranks:
                parts = [ans[q][r][goals[r, k, lax.rem(i, per) * nb + b]] for k in range(HG)]
                cols = slice((r % 2) * QUART * DV, (r % 2 + 1) * QUART * DV)
                for t in range(QUART):
                    tile = parts[(QUART - 1) ^ t]
                    for c in range(QUART - 1):
                        tile = jnp.where(group_at == c, parts[c ^ t], tile)
                    mixing[r // 2][t, b, :, cols] = tile
            return carry

        lax.fori_loop(0, nb, one, 0)

    def mixed_in(q, c, t):
        return jnp.dot(mixing[c][t].reshape(nb * QROWS, depth), wo_part[q, t, c * depth:(c + 1) * depth],
                       preferred_element_type=jnp.float32)

    def finish_first():
        assemble(0, range(HG))
        for t in range(QUART):
            base = own[t].reshape(nb * QROWS, width).astype(jnp.float32)
            acc[t] = base + mixed_in(0, 0, t) + mixed_in(0, 1, t)

    def finish_near():
        assemble(1, (0, 1))
        for t in range(QUART):
            acc[t] += mixed_in(1, 0, t)

    def finish_last():
        assemble(1, (3,))
        for t in range(QUART):
            out[:, t * QROWS:(t + 1) * QROWS] = (acc[t] + mixed_in(1, 1, t)).astype(jnp.bfloat16).reshape(
                nb, QROWS, width)

    def each(body, first=1, last=n):
        def one(p, carry):
            odd = lax.rem(p, 2)
            body(odd * lax.div(p + 1, 2) + (1 - odd) * (n - lax.div(p, 2)))
            return carry

        lax.fori_loop(first, last, one, 0)

    def first_values(p):
        take_v(0, source(p))
        send_v(1, p).start()
        ready_v_of(0, source(p))

    def second_values(p):
        take_v(1, source(p))
        ready_v_of(1, source(p))

    for c in range(PARTS):
        over_x(c).wait_send()
        over_core(c).wait_send()
        onward(c).wait_send()
        shared_sent(c)
    for copy in goal_copies:
        copy.wait_send()
    each(first_values)
    pass_tail(0)
    ready_v_of(1, i)
    tail_s.wait_send()
    take_tail(0)
    own_answer(0)
    each(lambda p: answer(0, p))
    values_sent(0)
    mid = n // 2 + 1
    each(second_values)
    pass_tail(1)
    each(lambda p: relay(0, p), 1, mid)
    take_tail(1)
    own_answer(1)
    each(lambda p: answer(1, p))
    each(lambda p: relay(0, p), mid)
    relay1(0).start()
    values_sent(1)

    def turn_over(p):
        relay(1, p)

    each(turn_over, 1, mid)
    spread(0)
    each(turn_over, mid)
    relay1(1).start()
    replies_sent(0)
    relay1(0).wait_recv()
    relay3(0).wait_recv()
    finish_first()
    relay1(1).wait_recv()
    finish_near()
    spread(1)
    assemble(1, (2,))
    relays_sent(0)
    replies_sent(1)
    for q in range(HALVES):
        tail_v(q).wait_send()
    relay3(1).wait_recv()
    finish_last()
    relays_sent(1)


def per_device(tokens, buckets, w_shared, w_value, w_output):
    n = lax.axis_size("seq")
    nb = buckets.shape[0]
    rows, width = tokens.shape
    cap = max(1, nb * HG // n)
    slots = n * cap
    bf = jnp.bfloat16
    vmem = pl.BlockSpec(memory_space=pltpu.VMEM)
    tiles = n * nb // LANES
    i32 = jnp.int32
    square = pltpu.VMEM((tiles, HG, LANES, LANES), i32)
    line = pltpu.VMEM((tiles, 8, LANES), i32)
    hbm = pl.BlockSpec(memory_space=pltpu.HBM)
    dma = lambda *k: pltpu.SemaphoreType.DMA(k)
    gathered = pltpu.VMEM((PARTS, nb, ROWS, width), bf)
    weight = pltpu.VMEM(w_shared.shape, bf)
    small = (FOLD, 2 * DH)
    quarter = (QROWS, QUART * DV)
    out = pl.pallas_call(
        functools.partial(main_kernel, n, cap, nb),
        out_shape=jax.ShapeDtypeStruct((nb, BLK, width), bf),
        in_specs=[hbm] * 5,
        out_specs=vmem,
        scratch_shapes=[pltpu.VMEM((HG, nb), i32), pltpu.VMEM((8, LANES), i32), pltpu.VMEM((n, 8, LANES), i32)]
        + [square] * 2 + [line] * 2
        + [pltpu.VMEM((8, LANES), i32), pltpu.SMEM((8, LANES), i32)]
        + [pltpu.VMEM((HG, 8, LANES), i32), pltpu.SMEM((HG, 8, LANES), i32)]
        + [gathered] + [weight] * 3
        + [pltpu.VMEM((HALVES, QUART, HG * QUART * DV, width), bf), pltpu.VMEM((QUART * DV, QUART * QUART * DV), bf)]
        + [gathered] * 3
        + [pltpu.VMEM((PARTS, nb * HG) + small, bf), pltpu.VMEM((nb, BLK, HG * DH), bf)]
        + [pltpu.VMEM((HALVES, nb * HG) + quarter, bf)]
        + [pltpu.VMEM((PARTS, n, cap) + small, bf), pltpu.VMEM((HALVES, n, cap) + quarter, bf)]
        + [pltpu.VMEM((PARTS, slots) + small, bf)] + [pltpu.VMEM((slots,) + quarter, bf)] * 2
        + [pltpu.VMEM((HG, PARTS) + small, bf)] * 2
        + [pltpu.VMEM((HALVES, HG) + quarter, bf)] * 2
        + [pltpu.VMEM((slots + HG, BLK, 2 * DH), bf)] * 3
        + [pltpu.VMEM((slots, BLK, 2 * BLK), bf)]
        + [pltpu.VMEM((HALVES, n, cap) + quarter, bf)] + [pltpu.VMEM((slots,) + quarter, bf)] * (2 * HG)
        + [pltpu.VMEM((QUART, nb * QROWS, width), jnp.float32)]
        + [dma(PARTS), dma(4)] + [dma(HG)] * 2 + [dma(PARTS)] * 6 + [dma(PARTS), dma(PARTS, n), dma(HALVES), dma(HALVES, n)] + [dma(1 + HALVES)] * 2
        + [dma(HALVES, n)] * 2 + [dma(HALVES)] * 6,
        compiler_params=pltpu.CompilerParams(collective_id=0, has_side_effects=True,
                                             vmem_limit_bytes=62 << 20),
    )(buckets.T, tokens.reshape(nb, BLK, width), w_shared, w_value, w_output)
    return out.reshape(rows, width)


def solution(mesh):
    return jax.shard_map(
        per_device,
        mesh=mesh,
        in_specs=(
            P("seq", "head"),
            P("seq", "head"),
            P(None, "head"),
            P(None, "head"),
            P(None, "head"),
        ),
        out_specs=P("seq", "head"),
        check_vma=False,
    )
```

```python
import functools

import jax
import jax.numpy as jnp
from jax import lax
from jax.experimental import pallas as pl
from jax.experimental.pallas import tpu as pltpu
from jax.sharding import PartitionSpec as P

DH = 64
BLK = 128
HG = 4
LANES = 128
PARTS = 4
ROWS = BLK // PARTS
FOLD = ROWS // 2
HALVES = 2
DV = DH // HALVES
QUART = 4
QROWS = BLK // QUART
MESH = pl.DeviceIdType.MESH


def head_ring():
    g = lax.axis_index("head")
    h1 = g + 1 - 2 * lax.rem(g, 2)
    h2 = g + 2 - 4 * lax.div(g, 2)
    h3 = h1 + 2 - 4 * lax.div(h1, 2)
    return g, h1, h2, h3


def remote(src, dst, send, recv, seq, head):
    return pltpu.make_async_remote_copy(
        src_ref=src, dst_ref=dst, send_sem=send, recv_sem=recv,
        device_id=(seq, head), device_id_type=MESH,
    )


def greet(n, i, g, siblings):
    barrier = pltpu.get_barrier_semaphore()

    def say(p, c):
        pl.semaphore_signal(barrier, inc=1, device_id=(lax.rem(i + p, n), g), device_id_type=MESH)
        return c

    lax.fori_loop(1, n, say, 0)
    for h in siblings:
        pl.semaphore_signal(barrier, inc=1, device_id=(i, h), device_id_type=MESH)


def greeted(n):
    pl.semaphore_wait(pltpu.get_barrier_semaphore(), n + 2)


def rows_of(*parts):
    rows = list(parts)
    rows += [jnp.zeros_like(rows[0])] * (8 - len(rows))
    return jnp.concatenate(rows, axis=0)


def column_of(row):
    return jnp.transpose(jnp.broadcast_to(row, (LANES, LANES)))


def down(x):
    return jnp.sum(x, axis=0, keepdims=True)


def tables(n, nb, cap, i, ids, key_col, place_col, pos_row, target_row, tab):
    blocks, slots = n * nb, n * cap
    tiles = blocks // LANES
    per = LANES // nb
    lane = lax.broadcasted_iota(jnp.int32, (1, LANES), 1)
    across = lax.broadcasted_iota(jnp.int32, (LANES, LANES), 1)
    along = lax.broadcasted_iota(jnp.int32, (LANES, LANES), 0)
    earlier = along < across
    zero = jnp.zeros((1, LANES), jnp.int32)

    def keys(q, carry):
        total = ids[q * per]
        for o in range(1, per):
            total = total + ids[q * per + o]
        key = total * blocks + (q * LANES + lane)
        pos_row[q] = key
        for h in range(HG):
            key_col[q, h] = column_of(key[h:h + 1])
        return carry

    lax.fori_loop(0, tiles, keys, 0)

    def ranks(q, carry):
        key = pos_row[q]
        ranked = []
        for h in range(HG):
            def below(t, acc):
                return acc + down((key_col[t, h] < key[h:h + 1]).astype(jnp.int32))
            ranked.append(lax.fori_loop(0, tiles, below, zero))
        pos_row[q] = rows_of(*ranked)
        return carry

    lax.fori_loop(0, tiles, ranks, 0)

    def places(q, carry):
        inverse, code_at = carry
        pos = pos_row[q]
        owner = pos // nb
        src = (q * LANES + lane) // nb
        src_col = (q * LANES + along) // nb
        pair = owner + n * src
        pos_cols = [column_of(pos[h:h + 1]) for h in range(HG)]
        pair_cols = [p // nb + n * src_col for p in pos_cols]
        ks = []
        for h in range(HG):
            mine = pair[h:h + 1]
            k = down(((pair_cols[h] == mine) & earlier).astype(jnp.int32))
            for o in range(h):
                k = k + down((pair_cols[o] == mine).astype(jnp.int32))
            ks.append(k)
            k_col = column_of(k)
            place = jnp.where(pos_cols[h] // nb == i, src_col * cap + k_col, -1)
            code = pos_cols[h] + h * blocks
            place_col[q, h] = place
            key_col[q, h] = code
            code_at = code_at + down(jnp.where(place == across, code, 0))
            target = jnp.where(src_col == i, (pos_cols[h] // nb) * cap + k_col, -1)
            item = (along % nb) * HG + h
            inverse = inverse + down(jnp.where(target == across, item, 0))
        target_row[q] = jnp.minimum(owner * cap + rows_of(*ks), slots - 1)
        return inverse, code_at

    inverse, code_at = lax.fori_loop(0, tiles, places, (zero, zero))
    last_at = lane * blocks + i * nb + nb - 1

    def links(q, carry):
        before, tails = carry
        for h in range(HG):
            place, code = place_col[q, h], key_col[q, h]
            before = before + down(jnp.where((code == code_at - 1) & (place >= 0), place, 0))
            tails = tails + down(jnp.where((code == last_at) & (place >= 0), place, 0))
        return before, tails

    before, tails = lax.fori_loop(0, tiles, links, (zero, zero))
    before = jnp.where(code_at % nb == 0, slots + code_at // blocks, before)
    tab[...] = rows_of(jnp.minimum(inverse, nb * HG - 1), jnp.clip(before, 0, slots + HG - 1),
                       jnp.minimum(tails, slots - 1), jnp.clip(code_at // blocks, 0, HG - 1))


def main_kernel(n, cap, nb, buck_hbm, tok, ws_hbm, wv_hbm, wo_hbm, out,
                buck, sent, ids, key_col, place_col, pos_row, target_row, tab, idx, targets, goals,
                own, ws, wv, wo, wo_part, spread_v, g1, g2, g3, items_s, values, items_v, s_out, v_out,
                s_in, v_in0, v_in1, ts_out, ts_in, tv_out, tv_in, qbuf, kbuf, vbuf0, wbuf,
                out2, a00, a01, a02, a03, a10, a11, a12, a13, acc,
                local, wload, sg, rg, sx, rx, sc, rc, so, ro, ss, rs, sv, rv, st, rt,
                sr, rr, s1, r1, s2, r2, s3, r3):
    ans, v_in, vbuf = ((a00, a01, a02, a03), (a10, a11, a12, a13)), (v_in0, v_in1), (vbuf0, qbuf)
    i = lax.axis_index("seq")
    g, h1, h2, h3 = head_ring()
    width = tok.shape[-1]
    slots = n * cap

    def part_of(c):
        return tok.at[:, pl.ds(c * ROWS, ROWS), :]

    loads = [pltpu.make_async_copy(src, dst, wload.at[k])
             for k, (src, dst) in enumerate(((ws_hbm, ws), (wv_hbm, wv), (wo_hbm, wo)))]
    own_loads = [pltpu.make_async_copy(part_of(c), own.at[c], local.at[c]) for c in range(PARTS)]
    greet(n, i, g, (h1, h2, h3))
    fetch = pltpu.make_async_copy(buck_hbm, buck, wload.at[3])
    fetch.start()
    loads[0].start()
    for load in own_loads:
        load.start()
    loads[1].start()
    loads[2].start()
    per = LANES // nb
    sent[...] = jnp.zeros_like(sent)
    fetch.wait()
    sent[:HG, :nb] = buck[...]
    sent[...] = pltpu.roll(sent[...], lax.rem(i, per) * nb, 1)
    ids[i] = sent[...]
    greeted(n)

    def bucket_copy(p):
        peer = lax.rem(i + p, n)
        return remote(sent, ids.at[i], sr.at[0, peer], rr.at[0, i], peer, g)

    def x_part(c):
        return remote(part_of(c), g2.at[c], sx.at[c], rx.at[c], i, h2)

    x_part(0).start()

    def bucket_start(p, carry):
        bucket_copy(p).start()
        return carry

    lax.fori_loop(1, n, bucket_start, 0)

    def over_x(c):
        return remote(part_of(c), g2.at[c], sx.at[c], rx.at[c], i, h2)

    def over_core(c):
        return remote(part_of(c), g1.at[c], sc.at[c], rc.at[c], i, h1)

    def onward(c):
        return remote(g2.at[c], g3.at[c], so.at[c], ro.at[c], i, h1)


    over_core(0).start()
    for c in range(1, PARTS):
        over_x(c).start()
        over_core(c).start()

    def bucket_wait(p, carry):
        src = lax.rem(i + n - p, n)
        remote(sent, ids.at[src], sr.at[0, src], rr.at[0, src], src, g).wait()
        return carry

    lax.fori_loop(1, n, bucket_wait, 0)
    tables(n, nb, cap, i, ids, key_col, place_col, pos_row, target_row, tab)
    to_scalar = pltpu.make_async_copy(tab, idx, wload.at[3])
    to_scalar.start()
    targets[0] = target_row[lax.div(i, per)]
    goal_copies = [remote(targets.at[0], targets.at[r], sg.at[r], rg.at[r], i, h)
                   for r, h in ((1, h1), (2, h2), (3, h3))]
    for copy in goal_copies:
        copy.start()
    for load in loads:
        load.wait()
    for load in own_loads:
        load.wait()
    to_scalar.wait()

    def chunk(o):
        return pl.ds(o * cap, cap)

    def send_s(c, p):
        peer = lax.rem(i + p, n)
        return remote(s_out.at[c, peer], s_in.at[c, chunk(i)], ss.at[c], rs.at[c, i], peer, g)

    def send_v(q, p):
        peer = lax.rem(i + p, n)
        return remote(v_out.at[q, peer], v_in[q].at[chunk(i)], sv.at[q], rv.at[q, i], peer, g)

    low = lax.broadcasted_iota(jnp.int32, (FOLD, 2 * DH), 1) < DH
    group_at = lax.broadcasted_iota(jnp.int32, (QROWS, QUART * DV), 1) // DV
    query_scale = jnp.where(lax.broadcasted_iota(jnp.int32, (1, 2 * DH), 1) < DH,
                            jnp.float32(DH ** -0.5), jnp.float32(0.0))

    def unfold(x):
        x = x.astype(jnp.float32)
        turned = pltpu.roll(x, DH, 1)
        return jnp.concatenate([jnp.where(low, x, turned), jnp.where(low, turned, x)], axis=0)

    def khat_of(x):
        square = jnp.sum(x * x, axis=1, keepdims=True) * (0.5 / DH)
        return (x * lax.rsqrt(square + 1e-6)).astype(jnp.bfloat16)

    step_blocks = min(nb, 8)

    def project(c, w, store):
        def one(q, carry):
            total = jnp.zeros((step_blocks * ROWS, HG * DH), jnp.float32)
            for ref, h in ((own, g), (g1, h1), (g2, h2), (g3, h3)):
                x = ref[c, pl.ds(q * step_blocks, step_blocks)].reshape(step_blocks * ROWS, width)
                total += jnp.dot(x, w[pl.ds(pl.multiple_of(h * width, width), width), :],
                                 preferred_element_type=jnp.float32)
            store(c, q * step_blocks, total.astype(jnp.bfloat16))
            return carry

        lax.fori_loop(0, nb // step_blocks, one, 0)

    def store_s(c, at, full):
        for b in range(step_blocks):
            for h in range(HG):
                cols = slice(h * DH, (h + 1) * DH)
                items_s[c, (at + b) * HG + h] = jnp.concatenate(
                    [full[b * ROWS: b * ROWS + FOLD, cols],
                     full[b * ROWS + FOLD: (b + 1) * ROWS, cols]], axis=1)

    def store_v(c, at, full):
        values[pl.ds(at, step_blocks), pl.ds(pl.multiple_of(c * ROWS, ROWS), ROWS)] = (
            full.reshape(step_blocks, ROWS, HG * DH))

    def ready_s(c, o):
        rows = pl.ds(pl.multiple_of(c * ROWS, ROWS), ROWS)
        for k in range(cap):
            j = o * cap + k
            x = unfold(s_in[c, j])
            qbuf[j, rows] = (x * query_scale).astype(jnp.bfloat16)
            kbuf[j, rows] = khat_of(x)

    def arrive_s(c):
        ready_s(c, i)

        def one(p, carry):
            src = lax.rem(i + n - p, n)
            remote(s_out.at[c, src], s_in.at[c, chunk(src)], ss.at[c], rs.at[c, src], src, g).wait_recv()
            ready_s(c, src)
            return carry

        lax.fori_loop(1, n, one, 0)

    def gather(c, carry):
        over_x(c).wait_recv()
        onward(c).start()
        over_core(c).wait_recv()
        onward(c).wait_recv()
        project(c, ws, store_s)

        def pack(p, carry):
            peer = lax.rem(i + p, n)
            for k in range(cap):
                s_out[c, peer, k] = items_s[c, idx[0, peer * cap + k]]
            send_s(c, p).start()
            return carry

        lax.fori_loop(1, n, pack, 0)
        for k in range(cap):
            s_in[c, i * cap + k] = items_s[c, idx[0, i * cap + k]]
        project(c, wv, store_v)

        @pl.when(c > 0)
        def _():
            arrive_s(c - 1)
        return carry

    lax.fori_loop(0, PARTS, gather, 0)

    def build_v(q):
        def one(b, carry):
            for h in range(HG):
                cols = slice(h * DH + q * DV, h * DH + (q + 1) * DV)
                items_v[q, b * HG + h] = jnp.concatenate(
                    [values[b, t * QROWS:(t + 1) * QROWS, cols] for t in range(QUART)], axis=1)
            return carry

        lax.fori_loop(0, nb, one, 0)

        def pack(p, carry):
            peer = lax.rem(i + p, n)
            for k in range(cap):
                v_out[q, peer, k] = items_v[q, idx[0, peer * cap + k]]
            return carry

        lax.fori_loop(1, n, pack, 0)
        for k in range(cap):
            v_in[q][i * cap + k] = items_v[q, idx[0, i * cap + k]]

    build_v(0)

    def start_v(p, carry):
        send_v(0, p).start()
        return carry

    lax.fori_loop(1, n, start_v, 0)
    arrive_s(PARTS - 1)

    for h in range(HG):
        at = idx[2, h]
        for c in range(PARTS):
            ts_out[h, c] = s_in[c, at]
    following = lax.rem(i + 1, n)
    tail_s = remote(ts_out, ts_in, st.at[0], rt.at[0], following, g)
    tail_s.start()

    build_v(1)
    l_at = lax.broadcasted_iota(jnp.int32, (QUART * DV, QUART * QUART * DV), 0)
    w_at = lax.broadcasted_iota(jnp.int32, (QUART * DV, QUART * QUART * DV), 1)
    spread_v[...] = ((l_at // DV == w_at // (QUART * DV)) & (l_at % DV == w_at % DV)).astype(
        jnp.float32).astype(jnp.bfloat16)

    def ready_v(q, x, at, count):
        wide = jnp.dot(x.reshape(count * QROWS, QUART * DV), spread_v[...],
                       preferred_element_type=jnp.float32).astype(jnp.bfloat16)
        for t in range(QUART):
            vbuf[q][pl.ds(at, count), t * QROWS:(t + 1) * QROWS] = (
                wide[:, t * QUART * DV:(t + 1) * QUART * DV].reshape(count, QROWS, QUART * DV))

    def ready_v_of(q, o):
        ready_v(q, v_in[q][chunk(o)], o * cap, cap)

    ready_v_of(0, i)
    for r, h in enumerate((g, h1, h2, h3)):
        for q in range(HALVES):
            for t in range(QUART):
                for c in range(QUART):
                    src = pl.multiple_of(h * HG * DH, HG * DH) + (c ^ t) * DH + q * DV
                    wo_part[q, t, (r * QUART + c) * DV:(r * QUART + c + 1) * DV] = wo[pl.ds(src, DV), :]
    tail_s.wait_recv()
    for h in range(HG):
        for c in range(PARTS):
            kbuf[slots + h, c * ROWS:(c + 1) * ROWS] = khat_of(unfold(ts_in[h, c]))

    row_at = lax.broadcasted_iota(jnp.int32, (BLK, 2 * BLK), 0)
    col_at = lax.broadcasted_iota(jnp.int32, (BLK, 2 * BLK), 1)
    itself = col_at == row_at + BLK

    def weigh(o, carry):
        for k in range(cap):
            j = o * cap + k
            keys = jnp.concatenate([kbuf[idx[1, j]], kbuf[j]], axis=0)
            scores = lax.dot_general(qbuf[j], keys, (((1,), (1,)), ((), ())),
                                     preferred_element_type=jnp.float32)
            scores = jnp.where(itself, jnp.float32(-100000.0), scores)
            expo = jnp.exp(scores - jnp.max(scores, axis=1, keepdims=True))
            wbuf[j] = (expo * (1.0 / jnp.sum(expo, axis=1, keepdims=True))).astype(jnp.bfloat16)
        return carry

    lax.fori_loop(0, n, weigh, 0)
    for copy in goal_copies:
        copy.wait_recv()
    goal_scalar = pltpu.make_async_copy(targets, goals, wload.at[3])
    goal_scalar.start()

    def take_v(q, src):
        remote(v_out.at[q, src], v_in[q].at[chunk(src)], sv.at[q], rv.at[q, src], src, g).wait_recv()

    def pass_tail(q):
        for h in range(HG):
            tv_out[q, h] = v_in[q][idx[2, h]]
        tail_v(q).start()

    def take_tail(q):
        tail_v(q).wait_recv()
        ready_v(q, tv_in[q], slots, HG)

    def tail_v(q):
        return remote(tv_out.at[q], tv_in.at[q], st.at[1 + q], rt.at[1 + q], following, g)

    def attend(q, j):
        keyed = jnp.concatenate([vbuf[q][idx[1, j]], vbuf[q][j]], axis=0)
        mixed = jnp.dot(wbuf[j], keyed, preferred_element_type=jnp.float32)
        turn = group_at ^ idx[3, j]
        picked = mixed[(QUART - 1) * QROWS:]
        for t in range(QUART - 1):
            picked = jnp.where(turn == t, mixed[t * QROWS:(t + 1) * QROWS], picked)
        return picked.astype(jnp.bfloat16)

    def answers_of(e, r, o):
        return ans[e][r].at[chunk(o)]

    def reply(e, p):
        peer = lax.rem(i + p, n)
        return remote(out2.at[e, peer], answers_of(e, 0, i), sr.at[e, 0], rr.at[e, i], peer, g)

    def whole(e, r):
        return ans[e][r]

    def relay1(e):
        return remote(whole(e, 0), whole(e, 1), s1.at[e], r1.at[e], i, h1)

    def relay2(e, o):
        return remote(answers_of(e, 0, o), answers_of(e, 2, o), s2.at[e], r2.at[e], i, h2)

    def relay2_all(e):
        return remote(whole(e, 0), whole(e, 2), s2.at[e], r2.at[e], i, h2)

    def relay3(e):
        return remote(whole(e, 2), whole(e, 3), s3.at[e], r3.at[e], i, h1)

    def source(p):
        return lax.rem(i + n - p, n)

    def answer(q, p):
        peer = lax.rem(i + p, n)
        for k in range(cap):
            out2[q, peer, k] = attend(q, peer * cap + k)
        reply(q, p).start()

    def relay(e, p):
        src = source(p)
        remote(out2.at[e, src], answers_of(e, 0, src), sr.at[e, 0], rr.at[e, src], src, g).wait_recv()
        relay2(e, src).start()

    def spread(e):
        relay2_all(e).wait_recv()
        relay3(e).start()

    def own_answer(q):
        for k in range(cap):
            ans[q][0][i * cap + k] = attend(q, i * cap + k)
        relay2(q, i).start()

    def relays_sent(e):
        relay1(e).wait_send()
        relay2_all(e).wait_send()
        relay3(e).wait_send()

    following_peer = lax.rem(i + 1, n)

    def replies_sent(e):
        block = out2.at[e, pl.ds(0, n - 1)]
        remote(block, block, sr.at[e, 0], rr.at[e, 0], following_peer, g).wait_send()

    def values_sent(q):
        block = v_out.at[q, pl.ds(0, n - 1)]
        remote(block, block, sv.at[q], rv.at[q, 0], following_peer, g).wait_send()

    def shared_sent(c):
        block = s_out.at[c, pl.ds(0, n - 1)]
        remote(block, block, ss.at[c], rs.at[c, 0], following_peer, g).wait_send()

    goal_scalar.wait()
    mixing = (g1, g3)

    depth = 2 * QUART * DV

    def assemble(q, ranks):
        def one(b, carry):
            for r in ranks:
                parts = [ans[q][r][goals[r, k, lax.rem(i, per) * nb + b]] for k in range(HG)]
                cols = slice((r % 2) * QUART * DV, (r % 2 + 1) * QUART * DV)
                for t in range(QUART):
                    tile = parts[(QUART - 1) ^ t]
                    for c in range(QUART - 1):
                        tile = jnp.where(group_at == c, parts[c ^ t], tile)
                    mixing[r // 2][t, b, :, cols] = tile
            return carry

        lax.fori_loop(0, nb, one, 0)

    def mixed_in(q, c, t):
        return jnp.dot(mixing[c][t].reshape(nb * QROWS, depth), wo_part[q, t, c * depth:(c + 1) * depth],
                       preferred_element_type=jnp.float32)

    def finish_first():
        assemble(0, range(HG))
        for t in range(QUART):
            base = own[t].reshape(nb * QROWS, width).astype(jnp.float32)
            acc[t] = base + mixed_in(0, 0, t) + mixed_in(0, 1, t)

    def finish_near():
        assemble(1, (0, 1))
        for t in range(QUART):
            acc[t] += mixed_in(1, 0, t)

    def finish_last():
        assemble(1, (3,))
        for t in range(QUART):
            out[:, t * QROWS:(t + 1) * QROWS] = (acc[t] + mixed_in(1, 1, t)).astype(jnp.bfloat16).reshape(
                nb, QROWS, width)

    def each(body, first=1, last=n):
        def one(p, carry):
            odd = lax.rem(p, 2)
            body(odd * lax.div(p + 1, 2) + (1 - odd) * (n - lax.div(p, 2)))
            return carry

        lax.fori_loop(first, last, one, 0)

    def first_values(p):
        take_v(0, source(p))
        ready_v_of(0, source(p))

    def second_values(p):
        take_v(1, source(p))
        ready_v_of(1, source(p))

    for c in range(PARTS):
        over_x(c).wait_send()
        over_core(c).wait_send()
        onward(c).wait_send()
        shared_sent(c)
    for copy in goal_copies:
        copy.wait_send()
    each(lambda p: send_v(1, p).start())
    each(first_values)
    pass_tail(0)
    ready_v_of(1, i)
    tail_s.wait_send()
    take_tail(0)
    own_answer(0)
    each(lambda p: answer(0, p))
    values_sent(0)
    mid = n // 2 + 1
    each(second_values)
    pass_tail(1)
    each(lambda p: relay(0, p), 1, mid)
    take_tail(1)
    own_answer(1)
    each(lambda p: answer(1, p), 1, mid)
    each(lambda p: relay(0, p), mid)
    each(lambda p: answer(1, p), mid)
    relay1(0).start()
    values_sent(1)

    def turn_over(p):
        relay(1, p)

    each(turn_over, 1, mid)
    spread(0)
    each(turn_over, mid)
    relay1(1).start()
    replies_sent(0)
    relay1(0).wait_recv()
    relay3(0).wait_recv()
    finish_first()
    relay1(1).wait_recv()
    finish_near()
    spread(1)
    assemble(1, (2,))
    relays_sent(0)
    replies_sent(1)
    for q in range(HALVES):
        tail_v(q).wait_send()
    relay3(1).wait_recv()
    finish_last()
    relays_sent(1)


def per_device(tokens, buckets, w_shared, w_value, w_output):
    n = lax.axis_size("seq")
    nb = buckets.shape[0]
    rows, width = tokens.shape
    cap = max(1, nb * HG // n)
    slots = n * cap
    bf = jnp.bfloat16
    vmem = pl.BlockSpec(memory_space=pltpu.VMEM)
    tiles = n * nb // LANES
    i32 = jnp.int32
    square = pltpu.VMEM((tiles, HG, LANES, LANES), i32)
    line = pltpu.VMEM((tiles, 8, LANES), i32)
    hbm = pl.BlockSpec(memory_space=pltpu.HBM)
    dma = lambda *k: pltpu.SemaphoreType.DMA(k)
    gathered = pltpu.VMEM((PARTS, nb, ROWS, width), bf)
    weight = pltpu.VMEM(w_shared.shape, bf)
    small = (FOLD, 2 * DH)
    quarter = (QROWS, QUART * DV)
    out = pl.pallas_call(
        functools.partial(main_kernel, n, cap, nb),
        out_shape=jax.ShapeDtypeStruct((nb, BLK, width), bf),
        in_specs=[hbm] * 5,
        out_specs=vmem,
        scratch_shapes=[pltpu.VMEM((HG, nb), i32), pltpu.VMEM((8, LANES), i32), pltpu.VMEM((n, 8, LANES), i32)]
        + [square] * 2 + [line] * 2
        + [pltpu.VMEM((8, LANES), i32), pltpu.SMEM((8, LANES), i32)]
        + [pltpu.VMEM((HG, 8, LANES), i32), pltpu.SMEM((HG, 8, LANES), i32)]
        + [gathered] + [weight] * 3
        + [pltpu.VMEM((HALVES, QUART, HG * QUART * DV, width), bf), pltpu.VMEM((QUART * DV, QUART * QUART * DV), bf)]
        + [gathered] * 3
        + [pltpu.VMEM((PARTS, nb * HG) + small, bf), pltpu.VMEM((nb, BLK, HG * DH), bf)]
        + [pltpu.VMEM((HALVES, nb * HG) + quarter, bf)]
        + [pltpu.VMEM((PARTS, n, cap) + small, bf), pltpu.VMEM((HALVES, n, cap) + quarter, bf)]
        + [pltpu.VMEM((PARTS, slots) + small, bf)] + [pltpu.VMEM((slots,) + quarter, bf)] * 2
        + [pltpu.VMEM((HG, PARTS) + small, bf)] * 2
        + [pltpu.VMEM((HALVES, HG) + quarter, bf)] * 2
        + [pltpu.VMEM((slots + HG, BLK, 2 * DH), bf)] * 3
        + [pltpu.VMEM((slots, BLK, 2 * BLK), bf)]
        + [pltpu.VMEM((HALVES, n, cap) + quarter, bf)] + [pltpu.VMEM((slots,) + quarter, bf)] * (2 * HG)
        + [pltpu.VMEM((QUART, nb * QROWS, width), jnp.float32)]
        + [dma(PARTS), dma(4)] + [dma(HG)] * 2 + [dma(PARTS)] * 6 + [dma(PARTS), dma(PARTS, n), dma(HALVES), dma(HALVES, n)] + [dma(1 + HALVES)] * 2
        + [dma(HALVES, n)] * 2 + [dma(HALVES)] * 6,
        compiler_params=pltpu.CompilerParams(collective_id=0, has_side_effects=True,
                                             vmem_limit_bytes=62 << 20),
    )(buckets.T, tokens.reshape(nb, BLK, width), w_shared, w_value, w_output)
    return out.reshape(rows, width)


def solution(mesh):
    return jax.shard_map(
        per_device,
        mesh=mesh,
        in_specs=(
            P("seq", "head"),
            P("seq", "head"),
            P(None, "head"),
            P(None, "head"),
            P(None, "head"),
        ),
        out_specs=P("seq", "head"),
        check_vma=False,
    )
```
